32 devices in a mesh: orow: 8 (over z, x), ocol: 4 (over y, core).
Axes of the slice: x: 2, y: 2, z: 4, core: 2. Of those that a mesh axis runs over, the one named last changes fastest.
Arguments:
- integrals: bfloat16 [2304, 16, 384], P('ocol', 'orow'), may hold values from -0.29882812 to 0.29882812
- occ_count: int32 [8], replicated, may hold values from 1 to 2
- occ_energy: float32 [16], replicated, may hold values from -2 to -0.5
- vir_energy: float32 [384], replicated, may hold values from 0.3 to 2.5
- task_iblock: int32 [32, 1], replicated, may hold values from 0 to 7; in each aligned block of 32 rows (0 to 31, 32 to 63, ...) at most 8 rows name the same one
- task_jblock: int32 [32], replicated, may hold values from 0 to 7
Outputs:
- gamma_out: float32 [2304, 16, 384], P('ocol', 'orow')
- density: float32 [384, 384], replicated
The draws below stay inside these ranges and needn't reach their ends.
Inputs may be any that keep to these rules, and one draw needn't show every extreme that they name: `task_iblock`: no first block is named by more than 8 tasks, and some first block by exactly 8.
All inputs are finite; a program needn't handle non-finite values.
Results may differ from the reference program's by a relative error of at most 0.0019.
Values may be sent and summed in bfloat16 or wider, within the bound.
A program may use at most 128 MiB of HBM per device.

```python
import math
import jax
import jax.numpy as jnp
import numpy as np
from jax import lax

NAUX = 2304
NVIR = 384
OB = 2
MOST = 8
TASKS = 32
OCC = 16
N_OROW = 8


def with_ends(result, stream_key, least, largest):
    extent = result.shape
    index_at = [jax.random.randint(jax.random.fold_in(stream_key, axis), (), 0, extent[axis]) for axis in range(len(extent))]
    result = result.at[tuple(index_at)].set(least)
    longest = extent.index(max(extent))
    index_at[longest] = (index_at[longest] + 1) % extent[longest]
    return result.at[tuple(index_at)].set(largest)


def block_levels(rng, dims, shards, low, top_value):
    loudness = 1.0
    for position, parts in shards:
        heights = jax.random.uniform(jax.random.fold_in(jax.random.fold_in(rng, 6), position), (parts,), jnp.float32, low / len(shards), top_value / len(shards))
        loudness = loudness * jnp.repeat(jnp.exp(heights), dims[position] // parts).reshape((-1,) + (1,) * (len(dims) - 1 - position))
    return loudness


def deal_out(rng, own, number, rows, count, top, reach, skew):
    order = jax.random.permutation(rng, count)
    crowded, ordinary = shares(count, rows * top, reach, skew, True), shares(count, rows * top, reach, skew, False)
    places = jnp.arange(count)

    def named(tallies, turn):
        used = int((tallies > 0).sum())
        fixed = max(1, used // 4)
        shifted = fixed + (places - fixed + turn * (used - fixed)) % max(1, count - fixed)
        return jnp.zeros((count,), jnp.int32).at[order[jnp.where(places < fixed, places, shifted)]].set(jnp.asarray(tallies, jnp.int32))

    tallies = jnp.where(number % 4 == 0, named(crowded, number // 4), named(ordinary, number - number // 4 - 1))
    mixed = jax.random.permutation(jax.random.fold_in(own, 3), count)
    source_of, taker = mixed[0:count // 2 * 2:2], mixed[1:count // 2 * 2:2]
    slack = jnp.minimum(tallies[source_of] - 1, reach - tallies[taker]) // 2
    slack = jnp.where((source_of == order[0]) | (taker == order[0]) | (tallies[taker] == 0), 0, jnp.maximum(slack, 0))
    shifted = jax.random.randint(jax.random.fold_in(own, 4), (count // 2,), 0, 1 << 20) % (slack + 1)
    tallies = tallies.at[source_of].add(-shifted).at[taker].add(shifted)
    items = jnp.searchsorted(jnp.cumsum(tallies), jnp.arange(rows * top), side="right").astype(jnp.int32)
    table = items.reshape(top, rows).T
    table = table[jax.random.permutation(jax.random.fold_in(own, 1), rows)]
    turn = jax.random.randint(jax.random.fold_in(own, 2), (rows, 1), 0, top)
    return jnp.take_along_axis(table, (jnp.arange(top)[None, :] + turn) % top, axis=1)


def shares(amount, total, most, lean, full):
    portions = [(1 << 20) // math.isqrt(grade ** lean) + 1 for grade in range(1, amount + 1)]
    largest = most if full else min(most, max(-(-total // amount), total * portions[0] // sum(portions)))
    least = 1 if total - largest >= amount - 1 else 0
    given, surplus = [largest] + [least] * (amount - 1), total - largest - least * (amount - 1)
    while surplus > 0:
        movable = [i for i in range(1, amount) if given[i] < largest] or [i for i in range(1, amount) if given[i] < most]
        pool, left = sum([portions[i] for i in movable]), surplus
        for i in movable:
            more = min(most - given[i], max(1, left * portions[i] // pool), surplus)
            given[i] = given[i] + more
            surplus = surplus - more
    return np.array(given)


def centred(stream_key, dims, scale, bound, pieces=(), kind=jnp.bfloat16):
    result = scale * jax.random.normal(stream_key, dims, jnp.float32)
    if pieces:
        result = result * block_levels(stream_key, dims, pieces, -0.22, 0.18)
    return jnp.clip(result, -bound, bound).astype(kind)


def setup_inputs(seed: int = 0) -> dict:
    key_list = jax.random.split(jax.random.key(seed), 7)
    integrals = centred(key_list[0], (NAUX, OCC, NVIR), 0.05, 0.29882812, ((0, 4), (1, 8)))
    occ_count = with_ends(jax.random.randint(key_list[1], (N_OROW,), 1, OB + 1), jax.random.fold_in(key_list[1], 1), 1, OB).astype(jnp.int32)
    occ_energy = jnp.clip(jax.random.uniform(key_list[2], (OCC,), jnp.float32, -2.0, -0.5), -2.0, -0.5)
    vir_energy = jnp.clip(jax.random.uniform(key_list[3], (NVIR,), jnp.float32, 0.3, 2.5), 0.3, 2.5)
    task_iblock_keys = jax.random.split(jax.random.fold_in(key_list[4], 1), TASKS // TASKS)
    task_iblock_turns = jax.random.permutation(jax.random.fold_in(key_list[4], 3), TASKS // TASKS)
    task_iblock = jax.vmap(lambda own, number: deal_out(jax.random.fold_in(key_list[4], 2), own, number, TASKS, N_OROW, 1, MOST, 2))(task_iblock_keys, task_iblock_turns).reshape((TASKS, 1))
    task_jblock = with_ends(jax.random.randint(key_list[5], (TASKS,), 0, N_OROW), jax.random.fold_in(key_list[5], 1), 0, N_OROW - 1).astype(jnp.int32)
    return {"integrals": integrals, "occ_count": occ_count, "occ_energy": occ_energy, "vir_energy": vir_energy, "task_iblock": task_iblock, "task_jblock": task_jblock}


def amplitude(k_total, i_energy, j_energy, vir_energy):
    orbitals = i_energy.shape[0]
    virtuals = vir_energy.shape[0]
    k_grid = k_total.reshape(orbitals, virtuals, orbitals, virtuals)
    denominator = (i_energy[:, None, None, None] + j_energy[None, None, :, None]
                   - vir_energy[None, :, None, None] - vir_energy[None, None, None, :])
    values = (2.0 * k_grid - jnp.swapaxes(k_grid, 1, 3)) / denominator
    return values.reshape(orbitals * virtuals, orbitals * virtuals)


def reference(integrals, occ_count, occ_energy, vir_energy, task_iblock, task_jblock):
    orbital_ids = jnp.arange(OCC, dtype=jnp.int32)
    active = (orbital_ids % OB) < occ_count[orbital_ids // OB]
    masked = integrals * active.astype(jnp.bfloat16)[None, :, None]
    flat_blocks = masked.reshape(NAUX, N_OROW, OB * NVIR)
    energy_grid = occ_energy.reshape(N_OROW, OB)

    def step(carry, pair):
        gamma_sum, dens_sum = carry
        first, second = pair
        i_rows = lax.dynamic_index_in_dim(flat_blocks, first, 1, keepdims=False)
        j_rows = lax.dynamic_index_in_dim(flat_blocks, second, 1, keepdims=False)
        k_total = jnp.dot(i_rows.T, j_rows, preferred_element_type=jnp.float32)
        i_energy = lax.dynamic_index_in_dim(energy_grid, first, 0, keepdims=False)
        j_energy = lax.dynamic_index_in_dim(energy_grid, second, 0, keepdims=False)
        amplitudes = amplitude(k_total, i_energy, j_energy, vir_energy).astype(jnp.bfloat16)
        gamma_i = jnp.dot(j_rows, amplitudes.T, preferred_element_type=jnp.float32)
        gamma_j = jnp.dot(i_rows, amplitudes, preferred_element_type=jnp.float32)
        gamma_sum = gamma_sum.at[:, first].add(gamma_i).at[:, second].add(gamma_j)
        grid = amplitudes.astype(jnp.float32).reshape(OB, NVIR, OB * NVIR)
        dens_sum = dens_sum + jnp.einsum('iaw,ibw->ab', grid, grid)
        return (gamma_sum, dens_sum), None

    start = (jnp.zeros((NAUX, N_OROW, OB * NVIR), jnp.float32), jnp.zeros((NVIR, NVIR), jnp.float32))
    pairs = (task_iblock[:, 0].astype(jnp.int32), task_jblock.astype(jnp.int32))
    (gamma_sum, dens_sum), _ = lax.scan(step, start, pairs)
    gamma_out = gamma_sum.reshape(NAUX, OCC, NVIR)
    density = dens_sum / TASKS
    return gamma_out, density
```

```python
import functools

import jax
import jax.numpy as jnp
from jax import lax
from jax.experimental import pallas as pl
from jax.experimental.pallas import tpu as pltpu
from jax.sharding import PartitionSpec as P

MESH = pl.DeviceIdType.MESH


def pair_kernel(orbitals, cols, num_ref, occ_ref, gr_ref, gs_ref, gc_ref, vrow_ref, vcol_ref, gamma_ref, dens_ref, flip_ref, amp_ref):
    s = pl.program_id(0)
    blocks = pl.num_programs(0)
    row, col = num_ref[0], num_ref[1]
    virtuals = vrow_ref.shape[1]

    @pl.when(s == 0)
    def _():
        gamma_ref[...] = jnp.zeros_like(gamma_ref)
        dens_ref[...] = jnp.zeros_like(dens_ref)
        flip_ref[...] = gr_ref[0].T

    touch = num_ref[2 + s]
    first = num_ref[2 + blocks + s]

    @pl.when(touch > 0)
    def _():
        weight = touch.astype(jnp.float32)
        for i in range(orbitals):
            own = pl.ds(i * virtuals, virtuals)
            k_rows = jnp.dot(flip_ref[own, :], gs_ref[0], preferred_element_type=jnp.float32)
            parts = []
            for j in range(orbitals):
                k_ij = k_rows[:, j * virtuals:(j + 1) * virtuals]
                pair = occ_ref[row * orbitals + i] + occ_ref[s * orbitals + j]
                denominator = (pair - vcol_ref[...]) - vrow_ref[...]
                parts.append(((2.0 * k_ij - k_ij.T) / denominator).astype(jnp.bfloat16))
            amp = jnp.concatenate(parts, axis=1)
            amp_ref[i] = amp
            gamma_ref[:, own] += weight * lax.dot_general(
                gc_ref[0], amp, (((1,), (1,)), ((), ())), preferred_element_type=jnp.float32)

        @pl.when(first > 0)
        def _():
            strip = virtuals // cols
            count = first.astype(jnp.float32)
            for i in range(orbitals):
                mine = amp_ref[i, pl.ds(pl.multiple_of(col * strip, strip), strip), :]
                dens_ref[...] += count * lax.dot_general(
                    mine, amp_ref[i], (((1,), (1,)), ((), ())), preferred_element_type=jnp.float32)


def density_kernel(scale, part_ref, out_ref, arrived, send_sem, take_sem, pass_sem, row_sem, fan_sem, col_sem):
    rows, cols = lax.axis_size("orow"), lax.axis_size("ocol")
    row, col = lax.axis_index("orow"), lax.axis_index("ocol")
    barrier = pltpu.get_barrier_semaphore()

    def peer(step):
        return lax.rem(row + step, rows)

    def other(step):
        return lax.rem(col + step, cols)

    @pl.loop(1, rows)
    def _(step):
        pl.semaphore_signal(barrier, inc=1, device_id={"orow": peer(step)}, device_id_type=MESH)

    @pl.loop(1, cols)
    def _(step):
        pl.semaphore_signal(barrier, inc=1, device_id={"ocol": other(step)}, device_id_type=MESH)

    pl.semaphore_wait(barrier, rows + cols - 2)

    def scatter(step):
        return pltpu.make_async_remote_copy(
            src_ref=part_ref.at[peer(step)], dst_ref=arrived.at[step - 1], send_sem=send_sem.at[step - 1],
            recv_sem=take_sem.at[step - 1], device_id={"orow": peer(step)}, device_id_type=MESH)

    def spread(step):
        spot = out_ref.at[col, row]
        return pltpu.make_async_remote_copy(
            src_ref=spot, dst_ref=spot, send_sem=pass_sem.at[step - 1],
            recv_sem=row_sem.at[step - 1], device_id={"orow": peer(step)}, device_id_type=MESH)

    def fan(step):
        spot = out_ref.at[col]
        return pltpu.make_async_remote_copy(
            src_ref=spot, dst_ref=spot, send_sem=fan_sem.at[step - 1],
            recv_sem=col_sem.at[step - 1], device_id={"ocol": other(step)}, device_id_type=MESH)

    @pl.loop(1, rows)
    def _(step):
        scatter(step).start()

    total = part_ref[row]
    for step in range(1, rows):
        scatter(step).wait()
        total = total + arrived[step - 1]
    out_ref[col, row] = total * scale

    @pl.loop(1, rows)
    def _(step):
        spread(step).start()

    @pl.loop(1, rows)
    def _(step):
        spread(step).wait()

    @pl.loop(1, cols)
    def _(step):
        fan(step).start()

    @pl.loop(1, cols)
    def _(step):
        fan(step).wait()


def sum_density(part, tasks):
    rows, cols = lax.axis_size("orow"), lax.axis_size("ocol")
    strip, virtuals = part.shape
    share = strip // rows
    full = pl.pallas_call(
        functools.partial(density_kernel, 1.0 / tasks),
        out_shape=jax.ShapeDtypeStruct((cols, rows, share, virtuals), jnp.float32),
        in_specs=[pl.BlockSpec(memory_space=pltpu.VMEM)],
        out_specs=pl.BlockSpec(memory_space=pltpu.VMEM),
        scratch_shapes=[
            pltpu.VMEM((rows - 1, share, virtuals), jnp.float32),
            pltpu.SemaphoreType.DMA((rows - 1,)),
            pltpu.SemaphoreType.DMA((rows - 1,)),
            pltpu.SemaphoreType.DMA((rows - 1,)),
            pltpu.SemaphoreType.DMA((rows - 1,)),
            pltpu.SemaphoreType.DMA((cols - 1,)),
            pltpu.SemaphoreType.DMA((cols - 1,)),
        ],
        compiler_params=pltpu.CompilerParams(collective_id=1, has_side_effects=True),
    )(part.reshape(rows, share, virtuals))
    return full.reshape(virtuals, virtuals)


def gather_kernel(nz, nx, ny, cut, shard_ref, all_ref, own_sem, send_sem, line_sem, pair_sem):
    aux_local = shard_ref.shape[0]
    row, col = lax.axis_index("orow"), lax.axis_index("ocol")
    z, x, y, k = row // nx, lax.rem(row, nx), col // 2, lax.rem(col, 2)
    spans = (pl.ds(0, cut), pl.ds(cut, aux_local - cut))

    def turn(at, by, extent):
        return lax.rem(at + by, extent)

    def place(dz=0, dx=0, dy=0):
        return turn(z, dz, nz) * nx + turn(x, dx, nx), turn(y, dy, ny)

    def device(dz=0, dx=0, dy=0, dk=0):
        r, c = place(dz, dx, dy)
        return {"orow": r, "ocol": c * 2 + lax.rem(k + dk, 2)}

    near = sorted(range(1, nz), key=lambda d: min(d, nz - d))
    lines = {
        "z": [dict(dz=d) for d in near],
        "x": [dict(dx=d) for d in range(1, nx)],
        "y": [dict(dy=d) for d in range(1, ny)],
    }
    peers = lines["z"] + lines["x"] + lines["y"] + [dict(dk=1)]
    barrier = pltpu.get_barrier_semaphore()
    for peer in peers:
        pl.semaphore_signal(barrier, inc=1, device_id=device(**peer), device_id_type=MESH)
    pl.semaphore_wait(barrier, len(peers))

    sent = []

    def push(piece, at, source, sem, peer):
        r, c = place(**at)
        copy = pltpu.make_async_remote_copy(
            src_ref=source, dst_ref=all_ref.at[r, c * 2 + k, spans[piece]], send_sem=send_sem.at[len(sent)],
            recv_sem=sem, device_id=device(**peer), device_id_type=MESH)
        copy.start()
        sent.append(copy)

    def pass_on(piece, at, order):
        r, c = place(**at)
        own = not at
        source = shard_ref.at[spans[piece]] if own else all_ref.at[r, c * 2 + k, spans[piece]]
        for axis in order:
            for peer in lines[axis]:
                push(piece, at, source, line_sem.at[piece, r, c], peer)
        push(piece, at, source, pair_sem.at[piece, r, c], dict(dk=1))

    def take(piece, at, sem, core):
        r, c = place(**at)
        spot = all_ref.at[r, c * 2 + core, spans[piece]]
        pltpu.make_async_remote_copy(
            src_ref=spot, dst_ref=spot, send_sem=send_sem.at[0], recv_sem=sem.at[piece, r, c],
            device_id=device(dk=1), device_id_type=MESH).wait_recv()

    def relay(piece, at, order):
        take(piece, at, line_sem, k)
        pass_on(piece, at, order)

    keep = pltpu.make_async_copy(shard_ref, all_ref.at[row, col], own_sem)
    keep.start()
    pass_on(1, {}, "yzx")
    pass_on(0, {}, "zxy")
    for side in lines["y"]:
        relay(1, side, "zx")
    for up in lines["z"]:
        relay(0, up, "xy")
    for up in [{}] + lines["z"]:
        for across in lines["x"]:
            relay(0, up | across, "y")
        if up:
            for side in [{}] + lines["y"]:
                relay(1, up | side, "x")
    for up in [{}] + lines["z"]:
        for across in [{}] + lines["x"]:
            for side in lines["y"]:
                relay(0, up | across | side, "")
        for side in [{}] + lines["y"]:
            for across in lines["x"]:
                relay(1, up | across | side, "")
    for dz in range(nz):
        for dx in range(nx):
            for dy in range(ny):
                for piece in (0, 1):
                    take(piece, dict(dz=dz, dx=dx, dy=dy), pair_sem, 1 - k)
    keep.wait()
    for copy in sent:
        copy.wait_send()


def gather_all(shard):
    rows, cols = lax.axis_size("orow"), lax.axis_size("ocol")
    ny = cols // 2
    nx = ny if rows % ny == 0 else 1
    nz = rows // nx
    aux_local, span = shard.shape
    cut = aux_local * 7 // 11 // 16 * 16
    pushes = 2 * nz * nx * ny + (nz - 1) + nz * (nx - 1) + nz * nx * (ny - 1) + (ny - 1) + ny * (nz - 1) + nz * ny * (nx - 1)
    return pl.pallas_call(
        functools.partial(gather_kernel, nz, nx, ny, cut),
        out_shape=jax.ShapeDtypeStruct((rows, cols, aux_local, span), shard.dtype),
        in_specs=[pl.BlockSpec(memory_space=pltpu.VMEM)],
        out_specs=pl.BlockSpec(memory_space=pl.ANY),
        scratch_shapes=[
            pltpu.SemaphoreType.DMA,
            pltpu.SemaphoreType.DMA((pushes,)),
            pltpu.SemaphoreType.DMA((2, rows, ny)),
            pltpu.SemaphoreType.DMA((2, rows, ny)),
        ],
        compiler_params=pltpu.CompilerParams(collective_id=2, has_side_effects=True),
    )(shard)


def fused_kernel(nz, nx, tasks, shard_ref, count_ref, occ_ref, ti_ref, tj_ref, vir_ref, out_ref, dens_ref,
                 mine, rows_ref, cols_ref, flip, vsum, amp, total, stage, xmsg, ymsg, keep, fold, part, gath, plane,
                 row_sem, col_sem, x_sem, y_sem, keep_sem, fold_sem, part_sem, plane_sem, dens_sem,
                 first_send, relay_send, pass_send, gamma_send, fold_send, part_send, plane_send, dens_send, home_sem):
    virtuals, aux = flip.shape
    row, col = lax.axis_index("orow"), lax.axis_index("ocol")
    z, x, y, k = row // nx, lax.rem(row, nx), col // 2, lax.rem(col, 2)
    nx_, ny_, nk_ = 1 - x, 1 - y, 1 - k
    owner = x == k
    other = jnp.logical_not(owner)
    both = jnp.logical_and
    dif = lax.rem(x + k, 2)
    block = z * nx + k
    cores = (k, nk_)

    def turn(by):
        return lax.rem(z + by + nz, nz)

    def device(dz, dx, dy, dk):
        return {"orow": dz * nx + dx, "ocol": dy * 2 + dk}

    def remote(src, dst, send, take, where):
        return pltpu.make_async_remote_copy(
            src_ref=src, dst_ref=dst, send_sem=send, recv_sem=take, device_id=where, device_id_type=MESH)

    up, down = turn(1), turn(-1)
    sibling = device(z, x, y, nk_)

    def arrive(ref, sem):
        remote(ref, ref, first_send.at[0], sem, sibling).wait_recv()

    barrier = pltpu.get_barrier_semaphore()
    peers = [sibling, device(z, x, ny_, 0), device(z, x, ny_, 1), device(z, nx_, y, 0), device(z, nx_, y, 1),
             device(z, nx_, ny_, k)]
    for d in range(1, nz):
        peers += [device(turn(d), x, y, 0), device(turn(d), x, y, 1)]
    for peer in peers:
        pl.semaphore_signal(barrier, inc=1, device_id=peer, device_id_type=MESH)

    count = count_ref[row]
    for r in range(2):
        o = lax.rem(y + r, 2)
        active = jnp.where(count > o, 1.0, 0.0).astype(jnp.float32)
        mine[r] = (shard_ref[o].astype(jnp.float32) * active).astype(jnp.bfloat16)
    cols_ref[0, 0] = mine[0]

    @pl.when(owner)
    def _():
        for r in range(2):
            rows_ref[r, 0] = mine[r]

    pl.semaphore_wait(barrier, len(peers))

    def give_row(source, r, q, where, slot):
        return remote(mine.at[source], rows_ref.at[r, q], first_send.at[slot], row_sem.at[r, q], where)

    def give_col(zr, q, where, slot):
        return remote(mine.at[0], cols_ref.at[zr, q], first_send.at[slot], col_sem.at[zr, q], where)

    opening = [
        give_row(1, 0, 2 + dif, device(z, x, ny_, x), 0),
        give_row(0, 0, dif, device(z, nx_, y, x), 1),
        give_col(1, 0, device(up, x, y, k), 2),
        give_col(2, 0, device(down, x, y, k), 3),
        give_col(0, 1, sibling, 4),
        give_row(0, 1, 2 + dif, device(z, x, ny_, x), 5),
    ]
    late = give_row(1, 1, dif, device(z, nx_, y, x), 6)
    home = [give_row(0, 0, 1, sibling, 7), give_row(1, 1, 1, sibling, 8)]
    for copy in opening:
        copy.start()

    @pl.when(other)
    def _():
        for copy in home:
            copy.start()

    def wait_row(r, q):
        arrive(rows_ref.at[r, q], row_sem.at[r, q])

    def wait_col(zr, q):
        arrive(cols_ref.at[zr, q], col_sem.at[zr, q])

    def relays(c):
        source = rows_ref.at[0, 2 + c]
        return [
            remote(source, cols_ref.at[1, 2], relay_send.at[c, 0], col_sem.at[1, 2], device(up, x, y, cores[c])),
            remote(source, cols_ref.at[2, 2], relay_send.at[c, 1], col_sem.at[2, 2], device(down, x, y, cores[c])),
            remote(source, rows_ref.at[0, 2 + c], relay_send.at[c, 2], row_sem.at[0, 2 + c], device(z, nx_, y, k)),
            remote(source, cols_ref.at[0, 3 - c], relay_send.at[c, 3], col_sem.at[0, 3 - c], sibling),
        ]

    def at_home(c):
        return pltpu.make_async_copy(rows_ref.at[0, 2 + c], cols_ref.at[0, 2 + c], home_sem.at[c])

    def across(c):
        return remote(rows_ref.at[0, c], rows_ref.at[1, 2 + c], relay_send.at[c, 0], row_sem.at[1, 2 + c],
                      device(z, x, ny_, k))

    @pl.when(owner)
    def _():
        for c in range(2):
            wait_row(0, 2 + c)
            for copy in relays(c):
                copy.start()
            at_home(c).start()

    @pl.when(other)
    def _():
        for c in range(2):
            wait_row(0, c)
            across(c).start()

    late.start()

    def tally(t, carry):
        a, b = ti_ref[t], tj_ref[t]
        result = []
        for zr, by in enumerate((0, -1, 1, 2)):
            j = turn(by) * nx + x
            ahead = jnp.where(a == block, 1, 0) * jnp.where(b == j, 1, 0)
            behind = jnp.where(b == block, 1, 0) * jnp.where(a == j, 1, 0)
            result += [carry[2 * zr] + ahead, carry[2 * zr + 1] + behind]
        return tuple(result)

    tallies = lax.fori_loop(0, tasks, tally, (jnp.int32(0),) * (2 * nz))
    ahead = [tallies[2 * zr].astype(jnp.float32) for zr in range(nz)]
    weight = [(tallies[2 * zr] + tallies[2 * zr + 1]).astype(jnp.float32) for zr in range(nz)]
    spread = jnp.broadcast_to(vir_ref[...], vsum.shape)
    vsum[...] = spread + spread.T

    before, beyond = 1 + k, 2 - k
    ahead_of = device(turn(1 - 2 * k), x, y, k)

    def pass_on(zr, a, slot):
        q = 2 * a
        return remote(cols_ref.at[zr, q], cols_ref.at[zr, q + 1], pass_send.at[slot], col_sem.at[zr, q + 1], sibling)

    passed = []

    def launch(copy):
        copy.start()
        passed.append(copy)

    def take_near(a):
        q = 2 * a
        wait_col(before, q)
        launch(remote(cols_ref.at[before, q], cols_ref.at[3, q], pass_send.at[len(passed)], col_sem.at[3, q], ahead_of))
        launch(pass_on(before, a, len(passed)))
        wait_col(beyond, q)
        launch(pass_on(beyond, a, len(passed)))

    def amplitudes(r, zr):
        kij = jnp.dot(flip[...], cols_ref[zr].reshape(aux, virtuals), preferred_element_type=jnp.float32)
        pair = occ_ref[block * 2 + lax.rem(y + r, 2)] + occ_ref[(turn((0, -1, 1, 2)[zr]) * nx + x) * 2 + y]
        amp[zr, r] = ((2.0 * kij - kij.T) / (pair - vsum[...])).astype(jnp.bfloat16)

    take_near(0)

    @pl.when(owner)
    def _():
        wait_row(0, 1)

    @pl.when(other)
    def _():
        for c in range(2):
            wait_row(0, 2 + c)

    flip[...] = rows_ref[0].reshape(aux, virtuals).T
    wait_col(0, 1)

    @pl.when(owner)
    def _():
        for c in range(2):
            at_home(c).wait()

    @pl.when(other)
    def _():
        for c in range(2):
            wait_col(0, 2 + c)

    amplitudes(0, 0)
    take_near(1)
    for zr in (1, 2):
        for q in (1, 3):
            wait_col(zr, q)
    for zr in (1, 2):
        amplitudes(0, zr)
    for a in range(2):
        wait_col(3, 2 * a)
        launch(pass_on(3, a, len(passed)))
    for q in (1, 3):
        wait_col(3, q)
    amplitudes(0, 3)

    def gamma_sends(r, a, c):
        zero, one = y == r, y == 1 - r
        q = 2 * a + c
        src, send = stage.at[r, q], gamma_send.at[r, q]
        if a == 0:
            sends = [(both(other, zero), remote(src, xmsg.at[r], send, x_sem.at[r], device(z, k, y, cores[c])))]
            if c == 1:
                sends.append((owner, remote(total.at[r, q], keep.at[r], send, keep_sem.at[r], sibling)))
            return sends
        return [
            (both(other, zero), remote(src, fold.at[c], send, fold_sem.at[c], device(z, k, y, k))),
            (both(other, one), remote(src, fold.at[c], send, fold_sem.at[c], device(z, x, ny_, k))),
            (both(owner, one), remote(src, ymsg.at[1 - r], send, y_sem.at[1 - r], device(z, x, ny_, cores[c]))),
        ]

    def guarded(condition, action):
        @pl.when(condition)
        def _():
            action()

    def gamma(r):
        for a in (1, 0):
            for c in range(2):
                q = 2 * a + c
                value = weight[0] * lax.dot_general(
                    cols_ref[0, q], amp[0, r], (((1,), (1,)), ((), ())), preferred_element_type=jnp.float32)
                for zr in range(1, nz):
                    value += weight[zr] * lax.dot_general(
                        cols_ref[zr, q], amp[zr, r], (((1,), (1,)), ((), ())), preferred_element_type=jnp.float32)
                total[r, q] = value
                stage[r, q] = value.astype(jnp.bfloat16)
                if q == 0:
                    @pl.when(owner)
                    def _():
                        keep[r] = value

                for condition, copy in gamma_sends(r, a, c):
                    guarded(condition, copy.start)

    def folded(own, r, c):
        if own:
            return remote(stage.at[r, 2 + c], ymsg.at[1 - r], fold_send.at[c], y_sem.at[1 - r], device(z, x, ny_, cores[c]))
        return remote(stage.at[r, c], xmsg.at[r], fold_send.at[c], x_sem.at[r], device(z, k, y, cores[c]))

    cases = [(True, 0, both(owner, y == 0)), (True, 1, both(owner, y == 1)),
             (False, 0, both(other, y == 1)), (False, 1, both(other, y == 0))]

    def fold_in(own, r, condition):
        @pl.when(condition)
        def _():
            for c in range(2):
                arrive(fold.at[c], fold_sem.at[c])
                q = (2 if own else 0) + c
                stage[r, q] = (total[r, q] + fold[c].astype(jnp.float32)).astype(jnp.bfloat16)
                folded(own, r, c).start()

    gamma(0)

    @pl.when(owner)
    def _():
        for q in (1, 2, 3):
            wait_row(1, q)

    @pl.when(other)
    def _():
        for q in range(4):
            wait_row(1, q)

    flip[...] = rows_ref[1].reshape(aux, virtuals).T
    for zr in range(nz):
        amplitudes(1, zr)
    fold_in(*cases[0])
    gamma(1)

    def square(zr):
        return sum(lax.dot_general(amp[zr, r], amp[zr, r], (((1,), (1,)), ((), ())),
                                   preferred_element_type=jnp.float32) for r in range(2))

    dens = ahead[0] * square(0)
    for zr in range(1, nz):
        dens += ahead[zr] * square(zr)
    part[...] = dens.reshape(part.shape)
    me = z * 2 + k
    ring = []
    for dz in range(nz):
        for dk in range(2):
            if dz or dk:
                tz, tk = turn(dz), lax.rem(k + dk, 2)
                ring.append((dz * 2 + dk, (nz - dz) % nz * 2 + dk, tz * 2 + tk, device(tz, x, y, tk)))

    def scatter(slot, back, there, where):
        return remote(part.at[there], gath.at[back], part_send.at[slot - 1], part_sem.at[back], where)

    for item in ring:
        scatter(*item).start()
    gath[0] = part[me]
    for case in cases[1:]:
        fold_in(*case)
    for slot, back, there, where in ring:
        arrive(gath.at[slot], part_sem.at[slot])
    strip = gath[0]
    for s in range(1, 2 * nz):
        strip = strip + gath[s]
    plane[0] = strip
    mates = [(1, device(z, nx_, y, k)), (2, device(z, x, ny_, k)), (3, device(z, nx_, ny_, k))]

    def swap(slot, where):
        return remote(plane.at[0], plane.at[slot], plane_send.at[slot - 1], plane_sem.at[slot], where)

    for mate in mates:
        swap(*mate).start()
    for slot, where in mates:
        arrive(plane.at[slot], plane_sem.at[slot])
    dens_ref[me] = ((plane[0] + plane[1]) + (plane[2] + plane[3])) * (1.0 / tasks)

    def spread_out(slot, back, there, where):
        return remote(dens_ref.at[me], dens_ref.at[me], dens_send.at[slot - 1], dens_sem.at[me], where)

    for item in ring:
        spread_out(*item).start()

    for r in range(2):
        guarded(other, lambda: arrive(keep.at[r], keep_sem.at[r]))
        arrive(xmsg.at[r], x_sem.at[r])
        arrive(ymsg.at[r], y_sem.at[r])
        out_ref[lax.rem(y + r, 2)] = (keep[r] + xmsg[r].astype(jnp.float32)) + ymsg[r].astype(jnp.float32)

    for slot, back, there, where in ring:
        arrive(dens_ref.at[there], dens_sem.at[there])
    for copy in opening + [late] + passed:
        copy.wait_send()

    @pl.when(other)
    def _():
        for copy in home:
            copy.wait_send()
        for c in range(2):
            across(c).wait_send()

    @pl.when(owner)
    def _():
        for c in range(2):
            for copy in relays(c):
                copy.wait_send()

    for r in range(2):
        for a in range(2):
            for c in range(2):
                for condition, copy in gamma_sends(r, a, c):
                    guarded(condition, copy.wait_send)
    for own, r, condition in cases:
        for c in range(2):
            guarded(condition, folded(own, r, c).wait_send)
    for item in ring:
        scatter(*item).wait_send()
        spread_out(*item).wait_send()
    for mate in mates:
        swap(*mate).wait_send()


def fused(integrals, occ_count, occ_energy, vir_energy, task_iblock, task_jblock, nz, nx):
    aux_local, orbitals, virtuals = integrals.shape
    aux = aux_local * lax.axis_size("ocol")
    tasks = task_jblock.shape[0]
    share = virtuals // (2 * nz)
    half, full = jnp.bfloat16, jnp.float32
    dma = pltpu.SemaphoreType.DMA
    vmem, smem = pl.BlockSpec(memory_space=pltpu.VMEM), pl.BlockSpec(memory_space=pltpu.SMEM)
    out, dens = pl.pallas_call(
        functools.partial(fused_kernel, nz, nx, tasks),
        out_shape=[
            jax.ShapeDtypeStruct((orbitals, aux_local, virtuals), full),
            jax.ShapeDtypeStruct((2 * nz, share, virtuals), full),
        ],
        in_specs=[vmem, smem, smem, smem, smem, vmem],
        out_specs=[vmem, vmem],
        scratch_shapes=[
            pltpu.VMEM((2, aux_local, virtuals), half),
            pltpu.VMEM((2, 4, aux_local, virtuals), half),
            pltpu.VMEM((nz, 4, aux_local, virtuals), half),
            pltpu.VMEM((virtuals, aux), half),
            pltpu.VMEM((virtuals, virtuals), full),
            pltpu.VMEM((nz, 2, virtuals, virtuals), half),
            pltpu.VMEM((2, 4, aux_local, virtuals), full),
            pltpu.VMEM((2, 4, aux_local, virtuals), half),
            pltpu.VMEM((2, aux_local, virtuals), half),
            pltpu.VMEM((2, aux_local, virtuals), half),
            pltpu.VMEM((2, aux_local, virtuals), full),
            pltpu.VMEM((2, aux_local, virtuals), half),
            pltpu.VMEM((2 * nz, share, virtuals), full),
            pltpu.VMEM((2 * nz, share, virtuals), full),
            pltpu.VMEM((4, share, virtuals), full),
            dma((2, 4)), dma((nz, 4)), dma((2,)), dma((2,)), dma((2,)), dma((2,)), dma((2 * nz,)), dma((4,)), dma((2 * nz,)),
            dma((9,)), dma((2, 4)), dma((8,)), dma((2, 4)), dma((2,)), dma((2 * nz - 1,)), dma((3,)), dma((2 * nz - 1,)), dma((2,)),
        ],
        compiler_params=pltpu.CompilerParams(
            collective_id=3, has_side_effects=True, vmem_limit_bytes=56 * 1024 * 1024),
    )(jnp.transpose(integrals, (1, 0, 2)), occ_count, occ_energy, task_iblock[:, 0], task_jblock, vir_energy[None, :])
    return jnp.transpose(out, (1, 0, 2)), dens.reshape(virtuals, virtuals)


def local(integrals, occ_count, occ_energy, vir_energy, task_iblock, task_jblock):
    aux_local, orbitals, virtuals = integrals.shape
    span = orbitals * virtuals
    blocks = lax.axis_size("orow")
    cols = lax.axis_size("ocol")
    if blocks == 8 and cols == 4 and orbitals == 2:
        return fused(integrals, occ_count, occ_energy, vir_energy, task_iblock, task_jblock, blocks // 2, 2)
    row = lax.axis_index("orow")
    col = lax.axis_index("ocol")
    aux = aux_local * cols
    active = jnp.arange(orbitals) < occ_count[row]
    masked = integrals * active.astype(jnp.bfloat16)[None, :, None]
    shard = masked.reshape(aux_local, span)
    gathered = gather_all(shard).reshape(blocks, aux, span)
    i_list, j_list = task_iblock[:, 0], task_jblock
    ids = jnp.arange(blocks)
    i_hot = i_list[None, :] == ids[:, None]
    j_hot = j_list[None, :] == ids[:, None]
    first = jnp.sum((i_list == row)[None, :] & j_hot, axis=1).astype(jnp.int32)
    second = jnp.sum((j_list == row)[None, :] & i_hot, axis=1).astype(jnp.int32)
    numbers = jnp.concatenate([jnp.stack([row, col]).astype(jnp.int32), first + second, first])
    gamma, dens = pl.pallas_call(
        functools.partial(pair_kernel, orbitals, cols),
        grid_spec=pltpu.PrefetchScalarGridSpec(
            num_scalar_prefetch=2,
            grid=(blocks,),
            in_specs=[
                pl.BlockSpec((1, aux, span), lambda s, num, occ: (num[0], 0, 0)),
                pl.BlockSpec((1, aux, span), lambda s, num, occ: (s, 0, 0)),
                pl.BlockSpec((1, aux_local, span), lambda s, num, occ: (s, num[1], 0)),
                pl.BlockSpec((1, virtuals), lambda s, num, occ: (0, 0)),
                pl.BlockSpec((virtuals, 1), lambda s, num, occ: (0, 0)),
            ],
            out_specs=[
                pl.BlockSpec((aux_local, span), lambda s, num, occ: (0, 0)),
                pl.BlockSpec((virtuals // cols, virtuals), lambda s, num, occ: (0, 0)),
            ],
            scratch_shapes=[pltpu.VMEM((span, aux), jnp.bfloat16), pltpu.VMEM((orbitals, virtuals, span), jnp.bfloat16)],
        ),
        out_shape=[
            jax.ShapeDtypeStruct((aux_local, span), jnp.float32),
            jax.ShapeDtypeStruct((virtuals // cols, virtuals), jnp.float32),
        ],
        compiler_params=pltpu.CompilerParams(vmem_limit_bytes=56 * 1024 * 1024),
    )(numbers, occ_energy, gathered, gathered, gathered, vir_energy[None, :], vir_energy[:, None])
    density = sum_density(dens, i_list.shape[0])
    return gamma.reshape(aux_local, orbitals, virtuals), density


def solution(mesh):
    return jax.shard_map(
        local,
        mesh=mesh,
        in_specs=(P("ocol", "orow", None), P(), P(), P(), P(), P()),
        out_specs=(P("ocol", "orow", None), P()),
        check_vma=False,
    )
```

```python
import functools

import jax
import jax.numpy as jnp
from jax import lax
from jax.experimental import pallas as pl
from jax.experimental.pallas import tpu as pltpu
from jax.sharding import PartitionSpec as P

MESH = pl.DeviceIdType.MESH


def pair_kernel(orbitals, cols, num_ref, occ_ref, gr_ref, gs_ref, gc_ref, vrow_ref, vcol_ref, gamma_ref, dens_ref, flip_ref, amp_ref):
    s = pl.program_id(0)
    blocks = pl.num_programs(0)
    row, col = num_ref[0], num_ref[1]
    virtuals = vrow_ref.shape[1]

    @pl.when(s == 0)
    def _():
        gamma_ref[...] = jnp.zeros_like(gamma_ref)
        dens_ref[...] = jnp.zeros_like(dens_ref)
        flip_ref[...] = gr_ref[0].T

    touch = num_ref[2 + s]
    first = num_ref[2 + blocks + s]

    @pl.when(touch > 0)
    def _():
        weight = touch.astype(jnp.float32)
        for i in range(orbitals):
            own = pl.ds(i * virtuals, virtuals)
            k_rows = jnp.dot(flip_ref[own, :], gs_ref[0], preferred_element_type=jnp.float32)
            parts = []
            for j in range(orbitals):
                k_ij = k_rows[:, j * virtuals:(j + 1) * virtuals]
                pair = occ_ref[row * orbitals + i] + occ_ref[s * orbitals + j]
                denominator = (pair - vcol_ref[...]) - vrow_ref[...]
                parts.append(((2.0 * k_ij - k_ij.T) / denominator).astype(jnp.bfloat16))
            amp = jnp.concatenate(parts, axis=1)
            amp_ref[i] = amp
            gamma_ref[:, own] += weight * lax.dot_general(
                gc_ref[0], amp, (((1,), (1,)), ((), ())), preferred_element_type=jnp.float32)

        @pl.when(first > 0)
        def _():
            strip = virtuals // cols
            count = first.astype(jnp.float32)
            for i in range(orbitals):
                mine = amp_ref[i, pl.ds(pl.multiple_of(col * strip, strip), strip), :]
                dens_ref[...] += count * lax.dot_general(
                    mine, amp_ref[i], (((1,), (1,)), ((), ())), preferred_element_type=jnp.float32)


def density_kernel(scale, part_ref, out_ref, arrived, send_sem, take_sem, pass_sem, row_sem, fan_sem, col_sem):
    rows, cols = lax.axis_size("orow"), lax.axis_size("ocol")
    row, col = lax.axis_index("orow"), lax.axis_index("ocol")
    barrier = pltpu.get_barrier_semaphore()

    def peer(step):
        return lax.rem(row + step, rows)

    def other(step):
        return lax.rem(col + step, cols)

    @pl.loop(1, rows)
    def _(step):
        pl.semaphore_signal(barrier, inc=1, device_id={"orow": peer(step)}, device_id_type=MESH)

    @pl.loop(1, cols)
    def _(step):
        pl.semaphore_signal(barrier, inc=1, device_id={"ocol": other(step)}, device_id_type=MESH)

    pl.semaphore_wait(barrier, rows + cols - 2)

    def scatter(step):
        return pltpu.make_async_remote_copy(
            src_ref=part_ref.at[peer(step)], dst_ref=arrived.at[step - 1], send_sem=send_sem.at[step - 1],
            recv_sem=take_sem.at[step - 1], device_id={"orow": peer(step)}, device_id_type=MESH)

    def spread(step):
        spot = out_ref.at[col, row]
        return pltpu.make_async_remote_copy(
            src_ref=spot, dst_ref=spot, send_sem=pass_sem.at[step - 1],
            recv_sem=row_sem.at[step - 1], device_id={"orow": peer(step)}, device_id_type=MESH)

    def fan(step):
        spot = out_ref.at[col]
        return pltpu.make_async_remote_copy(
            src_ref=spot, dst_ref=spot, send_sem=fan_sem.at[step - 1],
            recv_sem=col_sem.at[step - 1], device_id={"ocol": other(step)}, device_id_type=MESH)

    @pl.loop(1, rows)
    def _(step):
        scatter(step).start()

    total = part_ref[row]
    for step in range(1, rows):
        scatter(step).wait()
        total = total + arrived[step - 1]
    out_ref[col, row] = total * scale

    @pl.loop(1, rows)
    def _(step):
        spread(step).start()

    @pl.loop(1, rows)
    def _(step):
        spread(step).wait()

    @pl.loop(1, cols)
    def _(step):
        fan(step).start()

    @pl.loop(1, cols)
    def _(step):
        fan(step).wait()


def sum_density(part, tasks):
    rows, cols = lax.axis_size("orow"), lax.axis_size("ocol")
    strip, virtuals = part.shape
    share = strip // rows
    full = pl.pallas_call(
        functools.partial(density_kernel, 1.0 / tasks),
        out_shape=jax.ShapeDtypeStruct((cols, rows, share, virtuals), jnp.float32),
        in_specs=[pl.BlockSpec(memory_space=pltpu.VMEM)],
        out_specs=pl.BlockSpec(memory_space=pltpu.VMEM),
        scratch_shapes=[
            pltpu.VMEM((rows - 1, share, virtuals), jnp.float32),
            pltpu.SemaphoreType.DMA((rows - 1,)),
            pltpu.SemaphoreType.DMA((rows - 1,)),
            pltpu.SemaphoreType.DMA((rows - 1,)),
            pltpu.SemaphoreType.DMA((rows - 1,)),
            pltpu.SemaphoreType.DMA((cols - 1,)),
            pltpu.SemaphoreType.DMA((cols - 1,)),
        ],
        compiler_params=pltpu.CompilerParams(collective_id=1, has_side_effects=True),
    )(part.reshape(rows, share, virtuals))
    return full.reshape(virtuals, virtuals)


def gather_kernel(nz, nx, ny, cut, shard_ref, all_ref, own_sem, send_sem, line_sem, pair_sem):
    aux_local = shard_ref.shape[0]
    row, col = lax.axis_index("orow"), lax.axis_index("ocol")
    z, x, y, k = row // nx, lax.rem(row, nx), col // 2, lax.rem(col, 2)
    spans = (pl.ds(0, cut), pl.ds(cut, aux_local - cut))

    def turn(at, by, extent):
        return lax.rem(at + by, extent)

    def place(dz=0, dx=0, dy=0):
        return turn(z, dz, nz) * nx + turn(x, dx, nx), turn(y, dy, ny)

    def device(dz=0, dx=0, dy=0, dk=0):
        r, c = place(dz, dx, dy)
        return {"orow": r, "ocol": c * 2 + lax.rem(k + dk, 2)}

    near = sorted(range(1, nz), key=lambda d: min(d, nz - d))
    lines = {
        "z": [dict(dz=d) for d in near],
        "x": [dict(dx=d) for d in range(1, nx)],
        "y": [dict(dy=d) for d in range(1, ny)],
    }
    peers = lines["z"] + lines["x"] + lines["y"] + [dict(dk=1)]
    barrier = pltpu.get_barrier_semaphore()
    for peer in peers:
        pl.semaphore_signal(barrier, inc=1, device_id=device(**peer), device_id_type=MESH)
    pl.semaphore_wait(barrier, len(peers))

    sent = []

    def push(piece, at, source, sem, peer):
        r, c = place(**at)
        copy = pltpu.make_async_remote_copy(
            src_ref=source, dst_ref=all_ref.at[r, c * 2 + k, spans[piece]], send_sem=send_sem.at[len(sent)],
            recv_sem=sem, device_id=device(**peer), device_id_type=MESH)
        copy.start()
        sent.append(copy)

    def pass_on(piece, at, order):
        r, c = place(**at)
        own = not at
        source = shard_ref.at[spans[piece]] if own else all_ref.at[r, c * 2 + k, spans[piece]]
        for axis in order:
            for peer in lines[axis]:
                push(piece, at, source, line_sem.at[piece, r, c], peer)
        push(piece, at, source, pair_sem.at[piece, r, c], dict(dk=1))

    def take(piece, at, sem, core):
        r, c = place(**at)
        spot = all_ref.at[r, c * 2 + core, spans[piece]]
        pltpu.make_async_remote_copy(
            src_ref=spot, dst_ref=spot, send_sem=send_sem.at[0], recv_sem=sem.at[piece, r, c],
            device_id=device(dk=1), device_id_type=MESH).wait_recv()

    def relay(piece, at, order):
        take(piece, at, line_sem, k)
        pass_on(piece, at, order)

    keep = pltpu.make_async_copy(shard_ref, all_ref.at[row, col], own_sem)
    keep.start()
    pass_on(1, {}, "yzx")
    pass_on(0, {}, "zxy")
    for side in lines["y"]:
        relay(1, side, "zx")
    for up in lines["z"]:
        relay(0, up, "xy")
    for up in [{}] + lines["z"]:
        for across in lines["x"]:
            relay(0, up | across, "y")
        if up:
            for side in [{}] + lines["y"]:
                relay(1, up | side, "x")
    for up in [{}] + lines["z"]:
        for across in [{}] + lines["x"]:
            for side in lines["y"]:
                relay(0, up | across | side, "")
        for side in [{}] + lines["y"]:
            for across in lines["x"]:
                relay(1, up | across | side, "")
    for dz in range(nz):
        for dx in range(nx):
            for dy in range(ny):
                for piece in (0, 1):
                    take(piece, dict(dz=dz, dx=dx, dy=dy), pair_sem, 1 - k)
    keep.wait()
    for copy in sent:
        copy.wait_send()


def gather_all(shard):
    rows, cols = lax.axis_size("orow"), lax.axis_size("ocol")
    ny = cols // 2
    nx = ny if rows % ny == 0 else 1
    nz = rows // nx
    aux_local, span = shard.shape
    cut = aux_local * 7 // 11 // 16 * 16
    pushes = 2 * nz * nx * ny + (nz - 1) + nz * (nx - 1) + nz * nx * (ny - 1) + (ny - 1) + ny * (nz - 1) + nz * ny * (nx - 1)
    return pl.pallas_call(
        functools.partial(gather_kernel, nz, nx, ny, cut),
        out_shape=jax.ShapeDtypeStruct((rows, cols, aux_local, span), shard.dtype),
        in_specs=[pl.BlockSpec(memory_space=pltpu.VMEM)],
        out_specs=pl.BlockSpec(memory_space=pl.ANY),
        scratch_shapes=[
            pltpu.SemaphoreType.DMA,
            pltpu.SemaphoreType.DMA((pushes,)),
            pltpu.SemaphoreType.DMA((2, rows, ny)),
            pltpu.SemaphoreType.DMA((2, rows, ny)),
        ],
        compiler_params=pltpu.CompilerParams(collective_id=2, has_side_effects=True),
    )(shard)


def fused_kernel(nz, nx, tasks, shard_ref, count_ref, occ_ref, ti_ref, tj_ref, vir_ref, out_ref, dens_ref,
                 mine, rows_ref, cols_ref, flip, vsum, amp, total, stage, xmsg, ymsg, keep, fold, part, gath, strip, plane,
                 row_sem, col_sem, x_sem, y_sem, keep_sem, fold_sem, part_sem, plane_sem, line_sem, dens_sem,
                 first_send, relay_send, pass_send, gamma_send, fold_send, part_send, plane_send, col_send, dens_send, home_sem):
    virtuals, aux = flip.shape
    row, col = lax.axis_index("orow"), lax.axis_index("ocol")
    z, x, y, k = row // nx, lax.rem(row, nx), col // 2, lax.rem(col, 2)
    nx_, ny_, nk_ = 1 - x, 1 - y, 1 - k
    parity = lax.rem(z, 2)
    twin, mirror = z + 1 - 2 * parity, nz - 1 - z
    owner = parity == k
    other = jnp.logical_not(owner)
    both = jnp.logical_and
    dif = lax.rem(parity + k, 2)
    block = (z - parity + k) * nx + x
    cores = (k, nk_)

    def device(dz, dx, dy, dk):
        return {"orow": dz * nx + dx, "ocol": dy * 2 + dk}

    def remote(src, dst, send, take, where):
        return pltpu.make_async_remote_copy(
            src_ref=src, dst_ref=dst, send_sem=send, recv_sem=take, device_id=where, device_id_type=MESH)

    sibling = device(z, x, y, nk_)

    def arrive(ref, sem):
        remote(ref, ref, first_send.at[0], sem, sibling).wait_recv()

    barrier = pltpu.get_barrier_semaphore()
    peers = [sibling, device(nz - 1 - twin, x, y, k)]
    peers += [device(dz, x, ny_, k) for dz in (twin, mirror, nz - 1 - twin)]
    for c in range(2):
        peers += [device(z, x, ny_, c), device(z, nx_, y, c), device(twin, x, y, c), device(mirror, x, y, c)]
    for peer in peers:
        pl.semaphore_signal(barrier, inc=1, device_id=peer, device_id_type=MESH)

    count = count_ref[row]
    for r in range(2):
        o = lax.rem(y + r, 2)
        active = jnp.where(count > o, 1.0, 0.0).astype(jnp.float32)
        mine[r] = (shard_ref[o].astype(jnp.float32) * active).astype(jnp.bfloat16)
    cols_ref[0, 0] = mine[0]

    @pl.when(owner)
    def _():
        for r in range(2):
            rows_ref[r, 0] = mine[r]

    pl.semaphore_wait(barrier, len(peers))

    def give_row(source, r, q, where, slot):
        return remote(mine.at[source], rows_ref.at[r, q], first_send.at[slot], row_sem.at[r, q], where)

    def give_col(zr, q, where, slot):
        return remote(mine.at[0], cols_ref.at[zr, q], first_send.at[slot], col_sem.at[zr, q], where)

    opening = [
        give_row(1, 0, 2 + dif, device(z, x, ny_, parity), 0),
        give_col(2, 0, device(mirror, x, y, k), 3),
        give_col(1, 0, device(z, nx_, y, k), 2),
        give_row(1, 1, dif, device(twin, x, y, parity), 6),
        give_col(0, 1, sibling, 4),
        give_row(0, 1, 2 + dif, device(z, x, ny_, parity), 5),
        give_row(0, 0, dif, device(twin, x, y, parity), 1),
    ]
    home = [give_row(0, 0, 1, sibling, 7), give_row(1, 1, 1, sibling, 8)]
    for copy in opening:
        copy.start()

    @pl.when(other)
    def _():
        for copy in home:
            copy.start()

    def wait_row(r, q):
        arrive(rows_ref.at[r, q], row_sem.at[r, q])

    def wait_col(zr, q):
        arrive(cols_ref.at[zr, q], col_sem.at[zr, q])

    def relays(c):
        source = rows_ref.at[0, 2 + c]
        return [
            remote(source, cols_ref.at[2, 2], relay_send.at[c, 1], col_sem.at[2, 2], device(mirror, x, y, cores[c])),
            remote(source, cols_ref.at[1, 2], relay_send.at[c, 0], col_sem.at[1, 2], device(z, nx_, y, cores[c])),
            remote(source, cols_ref.at[0, 3 - c], relay_send.at[c, 3], col_sem.at[0, 3 - c], sibling),
        ]

    def at_home(c):
        return pltpu.make_async_copy(rows_ref.at[0, 2 + c], cols_ref.at[0, 2 + c], home_sem.at[c])

    def across(r, c):
        return remote(rows_ref.at[r, c], rows_ref.at[1 - r, 2 + c], relay_send.at[c, r], row_sem.at[1 - r, 2 + c],
                      device(z, x, ny_, k))

    @pl.when(owner)
    def _():
        for c in range(2):
            wait_row(0, 2 + c)
            for copy in relays(c):
                copy.start()
            at_home(c).start()

    @pl.when(other)
    def _():
        for r in (1, 0):
            for c in range(2):
                wait_row(r, c)
                across(r, c).start()

    places = (z * nx + x, z * nx + nx_, mirror * nx + x, mirror * nx + nx_)

    def tally(t, carry):
        a, b = ti_ref[t], tj_ref[t]
        result = []
        for zr, j in enumerate(places):
            ahead = jnp.where(a == block, 1, 0) * jnp.where(b == j, 1, 0)
            behind = jnp.where(b == block, 1, 0) * jnp.where(a == j, 1, 0)
            result += [carry[2 * zr] + ahead, carry[2 * zr + 1] + behind]
        return tuple(result)

    tallies = lax.fori_loop(0, tasks, tally, (jnp.int32(0),) * (2 * nz))
    ahead = [tallies[2 * zr].astype(jnp.float32) for zr in range(nz)]
    weight = [(tallies[2 * zr] + tallies[2 * zr + 1]).astype(jnp.float32) for zr in range(nz)]
    spread = jnp.broadcast_to(vir_ref[...].reshape(1, virtuals), vsum.shape)
    vsum[...] = spread + spread.T

    def pass_on(zr, a, slot):
        q = 2 * a
        return remote(cols_ref.at[zr, q], cols_ref.at[zr, q + 1], pass_send.at[slot], col_sem.at[zr, q + 1], sibling)

    passed = []

    def launch(copy):
        copy.start()
        passed.append(copy)

    def take(zr, a):
        q = 2 * a
        wait_col(zr, q)
        if zr == 2:
            launch(remote(cols_ref.at[2, q], cols_ref.at[3, q], pass_send.at[len(passed)], col_sem.at[3, q],
                          device(z, nx_, y, k)))
        launch(pass_on(zr, a, len(passed)))

    def amplitudes(r, zr):
        kij = jnp.dot(flip[...], cols_ref[zr].reshape(aux, virtuals), preferred_element_type=jnp.float32)
        pair = occ_ref[block * 2 + lax.rem(y + r, 2)] + occ_ref[places[zr] * 2 + y]
        amp[zr, r] = ((2.0 * kij - kij.T) / (pair - vsum[...])).astype(jnp.bfloat16)

    take(1, 0)
    take(2, 0)
    take(1, 1)

    @pl.when(owner)
    def _():
        wait_row(0, 1)

    @pl.when(other)
    def _():
        for c in range(2):
            wait_row(0, 2 + c)

    flip[...] = rows_ref[0].reshape(aux, virtuals).T
    wait_col(0, 1)

    @pl.when(owner)
    def _():
        for c in range(2):
            at_home(c).wait()

    @pl.when(other)
    def _():
        for c in range(2):
            wait_col(0, 2 + c)

    amplitudes(0, 0)
    take(2, 1)
    for q in (1, 3):
        wait_col(1, q)
    amplitudes(0, 1)
    take(3, 0)
    for q in (1, 3):
        wait_col(2, q)
    amplitudes(0, 2)
    take(3, 1)
    for q in (1, 3):
        wait_col(3, q)
    amplitudes(0, 3)

    def gamma_sends(r, a, c):
        zero, one = y == r, y == 1 - r
        q = 2 * a + c
        src, send = stage.at[r, q], gamma_send.at[r, q]
        if a == 0:
            sends = [(both(other, zero), remote(src, xmsg.at[r], send, x_sem.at[r], device(twin, x, y, cores[c])))]
            if c == 1:
                sends.append((owner, remote(total.at[r, q], keep.at[r], send, keep_sem.at[r], sibling)))
            return sends
        return [
            (both(other, zero), remote(src, fold.at[c], send, fold_sem.at[c], device(twin, x, y, k))),
            (both(other, one), remote(src, fold.at[c], send, fold_sem.at[c], device(z, x, ny_, k))),
            (both(owner, one), remote(src, ymsg.at[1 - r], send, y_sem.at[1 - r], device(z, x, ny_, cores[c]))),
        ]

    def guarded(condition, action):
        @pl.when(condition)
        def _():
            action()

    def send_off(r, a, c):
        for condition, copy in gamma_sends(r, a, c):
            guarded(condition, copy.start)

    def gamma(r, a, hold=False):
        for c in range(2):
            q = 2 * a + c
            value = weight[0] * lax.dot_general(
                cols_ref[0, q], amp[0, r], (((1,), (1,)), ((), ())), preferred_element_type=jnp.float32)
            for zr in range(1, nz):
                value += weight[zr] * lax.dot_general(
                    cols_ref[zr, q], amp[zr, r], (((1,), (1,)), ((), ())), preferred_element_type=jnp.float32)
            total[r, q] = value
            stage[r, q] = value.astype(jnp.bfloat16)
            if q == 0:
                @pl.when(owner)
                def _():
                    keep[r] = value

            if not hold:
                send_off(r, a, c)

    def folded(own, r, c):
        if own:
            return remote(stage.at[r, 2 + c], ymsg.at[1 - r], fold_send.at[c], y_sem.at[1 - r], device(z, x, ny_, cores[c]))
        return remote(stage.at[r, c], xmsg.at[r], fold_send.at[c], x_sem.at[r], device(twin, x, y, cores[c]))

    cases = [(True, 0, both(owner, y == 0)), (True, 1, both(owner, y == 1)),
             (False, 0, both(other, y == 1)), (False, 1, both(other, y == 0))]

    def fold_in(own, r, condition):
        @pl.when(condition)
        def _():
            for c in range(2):
                arrive(fold.at[c], fold_sem.at[c])
                q = (2 if own else 0) + c
                stage[r, q] = (total[r, q] + fold[c].astype(jnp.float32)).astype(jnp.bfloat16)
                folded(own, r, c).start()

    gamma(0, 1)

    @pl.when(owner)
    def _():
        for q in (1, 2, 3):
            wait_row(1, q)

    @pl.when(other)
    def _():
        for q in (2, 3):
            wait_row(1, q)

    flip[...] = rows_ref[1].reshape(aux, virtuals).T
    for zr in range(nz):
        amplitudes(1, zr)

    def square(zr):
        return sum(lax.dot_general(amp[zr, r], amp[zr, r], (((1,), (1,)), ((), ())),
                                   preferred_element_type=jnp.float32) for r in range(2))

    dens = ahead[0] * square(0)
    for zr in range(1, nz):
        dens += ahead[zr] * square(zr)
    part[...] = dens.reshape(part.shape)
    me = x * 2 + k
    quad = []
    for dx in range(2):
        for dk in range(2):
            if dx or dk:
                tx, tk = lax.rem(x + dx, 2), lax.rem(k + dk, 2)
                quad.append((dx * 2 + dk, tx * 2 + tk, device(z, tx, y, tk)))
    line = []
    for slot, dz in enumerate((z, twin, mirror, nz - 1 - twin)):
        for dy in range(2):
            if slot or dy:
                line.append((slot * 2 + dy, dz, device(dz, x, lax.rem(y + dy, 2), k)))

    def scatter(slot, there, where):
        return remote(part.at[there], gath.at[slot], part_send.at[slot - 1], part_sem.at[slot], where)

    def swap(slot, dz, where):
        return remote(strip.at[dz], plane.at[slot], plane_send.at[slot - 1], plane_sem.at[slot], where)

    def collect(slot, dz, where):
        return remote(dens_ref.at[me, z], dens_ref.at[me, z], col_send.at[slot // 2 - 1], line_sem.at[z], where)

    def spread_out(slot, there, where):
        return remote(dens_ref.at[me], dens_ref.at[me], dens_send.at[slot - 1], dens_sem.at[me], where)

    for item in quad:
        scatter(*item).start()
    gath[0] = part[me]
    gamma(0, 0, True)
    for slot, there, where in quad:
        arrive(gath.at[slot], part_sem.at[slot])
    strip[...] = (gath[0] + gath[1]) + (gath[2] + gath[3])
    for item in line:
        swap(*item).start()
    plane[0] = strip[z]
    for c in range(2):
        send_off(0, 0, c)
    fold_in(*cases[0])
    gamma(1, 1)
    for slot, dz, where in line:
        arrive(plane.at[slot], plane_sem.at[slot])
    dens_ref[me, z] = (((plane[0] + plane[1]) + (plane[2] + plane[3]))
                       + ((plane[4] + plane[5]) + (plane[6] + plane[7]))) * (1.0 / tasks)
    for item in line:
        if item[0] % 2 == 0:
            collect(*item).start()
    gamma(1, 0)
    for case in cases[1:]:
        fold_in(*case)
    for slot, dz, where in line:
        if slot % 2 == 0:
            arrive(dens_ref.at[me, dz], line_sem.at[dz])
    for item in quad:
        spread_out(*item).start()

    for r in range(2):
        guarded(other, lambda: arrive(keep.at[r], keep_sem.at[r]))
        arrive(xmsg.at[r], x_sem.at[r])
        arrive(ymsg.at[r], y_sem.at[r])
    for o in range(2):
        r = lax.rem(y + o, 2)
        out_ref[:, o, :] = (keep[r] + xmsg[r].astype(jnp.float32)) + ymsg[r].astype(jnp.float32)

    for slot, there, where in quad:
        arrive(dens_ref.at[there], dens_sem.at[there])
    for copy in opening + passed:
        copy.wait_send()

    @pl.when(other)
    def _():
        for copy in home:
            copy.wait_send()
        for r in range(2):
            for c in range(2):
                across(r, c).wait_send()

    @pl.when(owner)
    def _():
        for c in range(2):
            for copy in relays(c):
                copy.wait_send()

    for r in range(2):
        for a in range(2):
            for c in range(2):
                for condition, copy in gamma_sends(r, a, c):
                    guarded(condition, copy.wait_send)
    for own, r, condition in cases:
        for c in range(2):
            guarded(condition, folded(own, r, c).wait_send)
    for item in quad:
        scatter(*item).wait_send()
        spread_out(*item).wait_send()
    for item in line:
        swap(*item).wait_send()
        if item[0] % 2 == 0:
            collect(*item).wait_send()


def fused(integrals, occ_count, occ_energy, vir_energy, task_iblock, task_jblock, nz, nx):
    aux_local, orbitals, virtuals = integrals.shape
    aux = aux_local * lax.axis_size("ocol")
    tasks = task_jblock.shape[0]
    share = virtuals // (4 * nz)
    half, full = jnp.bfloat16, jnp.float32
    dma = pltpu.SemaphoreType.DMA
    vmem, smem = pl.BlockSpec(memory_space=pltpu.VMEM), pl.BlockSpec(memory_space=pltpu.SMEM)
    out, dens = pl.pallas_call(
        functools.partial(fused_kernel, nz, nx, tasks),
        out_shape=[
            jax.ShapeDtypeStruct((aux_local, orbitals, virtuals), full),
            jax.ShapeDtypeStruct((4, nz, share, virtuals), full),
        ],
        in_specs=[vmem, smem, smem, smem, smem, vmem],
        out_specs=[vmem, vmem],
        scratch_shapes=[
            pltpu.VMEM((2, aux_local, virtuals), half),
            pltpu.VMEM((2, 4, aux_local, virtuals), half),
            pltpu.VMEM((nz, 4, aux_local, virtuals), half),
            pltpu.VMEM((virtuals, aux), half),
            pltpu.VMEM((virtuals, virtuals), full),
            pltpu.VMEM((nz, 2, virtuals, virtuals), half),
            pltpu.VMEM((2, 4, aux_local, virtuals), full),
            pltpu.VMEM((2, 4, aux_local, virtuals), half),
            pltpu.VMEM((2, aux_local, virtuals), half),
            pltpu.VMEM((2, aux_local, virtuals), half),
            pltpu.VMEM((2, aux_local, virtuals), full),
            pltpu.VMEM((2, aux_local, virtuals), half),
            pltpu.VMEM((4, nz, share, virtuals), full),
            pltpu.VMEM((4, nz, share, virtuals), full),
            pltpu.VMEM((nz, share, virtuals), full),
            pltpu.VMEM((2 * nz, share, virtuals), full),
            dma((2, 4)), dma((nz, 4)), dma((2,)), dma((2,)), dma((2,)), dma((2,)), dma((4,)), dma((2 * nz,)), dma((nz,)), dma((4,)),
            dma((9,)), dma((2, 4)), dma((8,)), dma((2, 4)), dma((2,)), dma((3,)), dma((2 * nz - 1,)), dma((nz - 1,)), dma((3,)), dma((2,)),
        ],
        compiler_params=pltpu.CompilerParams(
            collective_id=3, has_side_effects=True, vmem_limit_bytes=56 * 1024 * 1024),
    )(jnp.transpose(integrals, (1, 0, 2)), occ_count, occ_energy, task_iblock[:, 0], task_jblock, vir_energy)
    return out, dens.reshape(virtuals, virtuals)


def local(integrals, occ_count, occ_energy, vir_energy, task_iblock, task_jblock):
    aux_local, orbitals, virtuals = integrals.shape
    span = orbitals * virtuals
    blocks = lax.axis_size("orow")
    cols = lax.axis_size("ocol")
    if blocks == 8 and cols == 4 and orbitals == 2:
        return fused(integrals, occ_count, occ_energy, vir_energy, task_iblock, task_jblock, blocks // 2, 2)
    row = lax.axis_index("orow")
    col = lax.axis_index("ocol")
    aux = aux_local * cols
    active = jnp.arange(orbitals) < occ_count[row]
    masked = integrals * active.astype(jnp.bfloat16)[None, :, None]
    shard = masked.reshape(aux_local, span)
    gathered = gather_all(shard).reshape(blocks, aux, span)
    i_list, j_list = task_iblock[:, 0], task_jblock
    ids = jnp.arange(blocks)
    i_hot = i_list[None, :] == ids[:, None]
    j_hot = j_list[None, :] == ids[:, None]
    first = jnp.sum((i_list == row)[None, :] & j_hot, axis=1).astype(jnp.int32)
    second = jnp.sum((j_list == row)[None, :] & i_hot, axis=1).astype(jnp.int32)
    numbers = jnp.concatenate([jnp.stack([row, col]).astype(jnp.int32), first + second, first])
    gamma, dens = pl.pallas_call(
        functools.partial(pair_kernel, orbitals, cols),
        grid_spec=pltpu.PrefetchScalarGridSpec(
            num_scalar_prefetch=2,
            grid=(blocks,),
            in_specs=[
                pl.BlockSpec((1, aux, span), lambda s, num, occ: (num[0], 0, 0)),
                pl.BlockSpec((1, aux, span), lambda s, num, occ: (s, 0, 0)),
                pl.BlockSpec((1, aux_local, span), lambda s, num, occ: (s, num[1], 0)),
                pl.BlockSpec((1, virtuals), lambda s, num, occ: (0, 0)),
                pl.BlockSpec((virtuals, 1), lambda s, num, occ: (0, 0)),
            ],
            out_specs=[
                pl.BlockSpec((aux_local, span), lambda s, num, occ: (0, 0)),
                pl.BlockSpec((virtuals // cols, virtuals), lambda s, num, occ: (0, 0)),
            ],
            scratch_shapes=[pltpu.VMEM((span, aux), jnp.bfloat16), pltpu.VMEM((orbitals, virtuals, span), jnp.bfloat16)],
        ),
        out_shape=[
            jax.ShapeDtypeStruct((aux_local, span), jnp.float32),
            jax.ShapeDtypeStruct((virtuals // cols, virtuals), jnp.float32),
        ],
        compiler_params=pltpu.CompilerParams(vmem_limit_bytes=56 * 1024 * 1024),
    )(numbers, occ_energy, gathered, gathered, gathered, vir_energy[None, :], vir_energy[:, None])
    density = sum_density(dens, i_list.shape[0])
    return gamma.reshape(aux_local, orbitals, virtuals), density


def solution(mesh):
    return jax.shard_map(
        local,
        mesh=mesh,
        in_specs=(P("ocol", "orow", None), P(), P(), P(), P(), P()),
        out_specs=(P("ocol", "orow", None), P()),
        check_vma=False,
    )
```

```python
import functools

import jax
import jax.numpy as jnp
from jax import lax
from jax.experimental import pallas as pl
from jax.experimental.pallas import tpu as pltpu
from jax.sharding import PartitionSpec as P

MESH = pl.DeviceIdType.MESH


def pair_kernel(orbitals, cols, num_ref, occ_ref, gr_ref, gs_ref, gc_ref, vrow_ref, vcol_ref, gamma_ref, dens_ref, flip_ref, amp_ref):
    s = pl.program_id(0)
    blocks = pl.num_programs(0)
    row, col = num_ref[0], num_ref[1]
    virtuals = vrow_ref.shape[1]

    @pl.when(s == 0)
    def _():
        gamma_ref[...] = jnp.zeros_like(gamma_ref)
        dens_ref[...] = jnp.zeros_like(dens_ref)
        flip_ref[...] = gr_ref[0].T

    touch = num_ref[2 + s]
    first = num_ref[2 + blocks + s]

    @pl.when(touch > 0)
    def _():
        weight = touch.astype(jnp.float32)
        for i in range(orbitals):
            own = pl.ds(i * virtuals, virtuals)
            k_rows = jnp.dot(flip_ref[own, :], gs_ref[0], preferred_element_type=jnp.float32)
            parts = []
            for j in range(orbitals):
                k_ij = k_rows[:, j * virtuals:(j + 1) * virtuals]
                pair = occ_ref[row * orbitals + i] + occ_ref[s * orbitals + j]
                denominator = (pair - vcol_ref[...]) - vrow_ref[...]
                parts.append(((2.0 * k_ij - k_ij.T) / denominator).astype(jnp.bfloat16))
            amp = jnp.concatenate(parts, axis=1)
            amp_ref[i] = amp
            gamma_ref[:, own] += weight * lax.dot_general(
                gc_ref[0], amp, (((1,), (1,)), ((), ())), preferred_element_type=jnp.float32)

        @pl.when(first > 0)
        def _():
            strip = virtuals // cols
            count = first.astype(jnp.float32)
            for i in range(orbitals):
                mine = amp_ref[i, pl.ds(pl.multiple_of(col * strip, strip), strip), :]
                dens_ref[...] += count * lax.dot_general(
                    mine, amp_ref[i], (((1,), (1,)), ((), ())), preferred_element_type=jnp.float32)


def density_kernel(scale, part_ref, out_ref, arrived, send_sem, take_sem, pass_sem, row_sem, fan_sem, col_sem):
    rows, cols = lax.axis_size("orow"), lax.axis_size("ocol")
    row, col = lax.axis_index("orow"), lax.axis_index("ocol")
    barrier = pltpu.get_barrier_semaphore()

    def peer(step):
        return lax.rem(row + step, rows)

    def other(step):
        return lax.rem(col + step, cols)

    @pl.loop(1, rows)
    def _(step):
        pl.semaphore_signal(barrier, inc=1, device_id={"orow": peer(step)}, device_id_type=MESH)

    @pl.loop(1, cols)
    def _(step):
        pl.semaphore_signal(barrier, inc=1, device_id={"ocol": other(step)}, device_id_type=MESH)

    pl.semaphore_wait(barrier, rows + cols - 2)

    def scatter(step):
        return pltpu.make_async_remote_copy(
            src_ref=part_ref.at[peer(step)], dst_ref=arrived.at[step - 1], send_sem=send_sem.at[step - 1],
            recv_sem=take_sem.at[step - 1], device_id={"orow": peer(step)}, device_id_type=MESH)

    def spread(step):
        spot = out_ref.at[col, row]
        return pltpu.make_async_remote_copy(
            src_ref=spot, dst_ref=spot, send_sem=pass_sem.at[step - 1],
            recv_sem=row_sem.at[step - 1], device_id={"orow": peer(step)}, device_id_type=MESH)

    def fan(step):
        spot = out_ref.at[col]
        return pltpu.make_async_remote_copy(
            src_ref=spot, dst_ref=spot, send_sem=fan_sem.at[step - 1],
            recv_sem=col_sem.at[step - 1], device_id={"ocol": other(step)}, device_id_type=MESH)

    @pl.loop(1, rows)
    def _(step):
        scatter(step).start()

    total = part_ref[row]
    for step in range(1, rows):
        scatter(step).wait()
        total = total + arrived[step - 1]
    out_ref[col, row] = total * scale

    @pl.loop(1, rows)
    def _(step):
        spread(step).start()

    @pl.loop(1, rows)
    def _(step):
        spread(step).wait()

    @pl.loop(1, cols)
    def _(step):
        fan(step).start()

    @pl.loop(1, cols)
    def _(step):
        fan(step).wait()


def sum_density(part, tasks):
    rows, cols = lax.axis_size("orow"), lax.axis_size("ocol")
    strip, virtuals = part.shape
    share = strip // rows
    full = pl.pallas_call(
        functools.partial(density_kernel, 1.0 / tasks),
        out_shape=jax.ShapeDtypeStruct((cols, rows, share, virtuals), jnp.float32),
        in_specs=[pl.BlockSpec(memory_space=pltpu.VMEM)],
        out_specs=pl.BlockSpec(memory_space=pltpu.VMEM),
        scratch_shapes=[
            pltpu.VMEM((rows - 1, share, virtuals), jnp.float32),
            pltpu.SemaphoreType.DMA((rows - 1,)),
            pltpu.SemaphoreType.DMA((rows - 1,)),
            pltpu.SemaphoreType.DMA((rows - 1,)),
            pltpu.SemaphoreType.DMA((rows - 1,)),
            pltpu.SemaphoreType.DMA((cols - 1,)),
            pltpu.SemaphoreType.DMA((cols - 1,)),
        ],
        compiler_params=pltpu.CompilerParams(collective_id=1, has_side_effects=True),
    )(part.reshape(rows, share, virtuals))
    return full.reshape(virtuals, virtuals)


def gather_kernel(nz, nx, ny, cut, shard_ref, all_ref, own_sem, send_sem, line_sem, pair_sem):
    aux_local = shard_ref.shape[0]
    row, col = lax.axis_index("orow"), lax.axis_index("ocol")
    z, x, y, k = row // nx, lax.rem(row, nx), col // 2, lax.rem(col, 2)
    spans = (pl.ds(0, cut), pl.ds(cut, aux_local - cut))

    def turn(at, by, extent):
        return lax.rem(at + by, extent)

    def place(dz=0, dx=0, dy=0):
        return turn(z, dz, nz) * nx + turn(x, dx, nx), turn(y, dy, ny)

    def device(dz=0, dx=0, dy=0, dk=0):
        r, c = place(dz, dx, dy)
        return {"orow": r, "ocol": c * 2 + lax.rem(k + dk, 2)}

    near = sorted(range(1, nz), key=lambda d: min(d, nz - d))
    lines = {
        "z": [dict(dz=d) for d in near],
        "x": [dict(dx=d) for d in range(1, nx)],
        "y": [dict(dy=d) for d in range(1, ny)],
    }
    peers = lines["z"] + lines["x"] + lines["y"] + [dict(dk=1)]
    barrier = pltpu.get_barrier_semaphore()
    for peer in peers:
        pl.semaphore_signal(barrier, inc=1, device_id=device(**peer), device_id_type=MESH)
    pl.semaphore_wait(barrier, len(peers))

    sent = []

    def push(piece, at, source, sem, peer):
        r, c = place(**at)
        copy = pltpu.make_async_remote_copy(
            src_ref=source, dst_ref=all_ref.at[r, c * 2 + k, spans[piece]], send_sem=send_sem.at[len(sent)],
            recv_sem=sem, device_id=device(**peer), device_id_type=MESH)
        copy.start()
        sent.append(copy)

    def pass_on(piece, at, order):
        r, c = place(**at)
        own = not at
        source = shard_ref.at[spans[piece]] if own else all_ref.at[r, c * 2 + k, spans[piece]]
        for axis in order:
            for peer in lines[axis]:
                push(piece, at, source, line_sem.at[piece, r, c], peer)
        push(piece, at, source, pair_sem.at[piece, r, c], dict(dk=1))

    def take(piece, at, sem, core):
        r, c = place(**at)
        spot = all_ref.at[r, c * 2 + core, spans[piece]]
        pltpu.make_async_remote_copy(
            src_ref=spot, dst_ref=spot, send_sem=send_sem.at[0], recv_sem=sem.at[piece, r, c],
            device_id=device(dk=1), device_id_type=MESH).wait_recv()

    def relay(piece, at, order):
        take(piece, at, line_sem, k)
        pass_on(piece, at, order)

    keep = pltpu.make_async_copy(shard_ref, all_ref.at[row, col], own_sem)
    keep.start()
    pass_on(1, {}, "yzx")
    pass_on(0, {}, "zxy")
    for side in lines["y"]:
        relay(1, side, "zx")
    for up in lines["z"]:
        relay(0, up, "xy")
    for up in [{}] + lines["z"]:
        for across in lines["x"]:
            relay(0, up | across, "y")
        if up:
            for side in [{}] + lines["y"]:
                relay(1, up | side, "x")
    for up in [{}] + lines["z"]:
        for across in [{}] + lines["x"]:
            for side in lines["y"]:
                relay(0, up | across | side, "")
        for side in [{}] + lines["y"]:
            for across in lines["x"]:
                relay(1, up | across | side, "")
    for dz in range(nz):
        for dx in range(nx):
            for dy in range(ny):
                for piece in (0, 1):
                    take(piece, dict(dz=dz, dx=dx, dy=dy), pair_sem, 1 - k)
    keep.wait()
    for copy in sent:
        copy.wait_send()


def gather_all(shard):
    rows, cols = lax.axis_size("orow"), lax.axis_size("ocol")
    ny = cols // 2
    nx = ny if rows % ny == 0 else 1
    nz = rows // nx
    aux_local, span = shard.shape
    cut = aux_local * 7 // 11 // 16 * 16
    pushes = 2 * nz * nx * ny + (nz - 1) + nz * (nx - 1) + nz * nx * (ny - 1) + (ny - 1) + ny * (nz - 1) + nz * ny * (nx - 1)
    return pl.pallas_call(
        functools.partial(gather_kernel, nz, nx, ny, cut),
        out_shape=jax.ShapeDtypeStruct((rows, cols, aux_local, span), shard.dtype),
        in_specs=[pl.BlockSpec(memory_space=pltpu.VMEM)],
        out_specs=pl.BlockSpec(memory_space=pl.ANY),
        scratch_shapes=[
            pltpu.SemaphoreType.DMA,
            pltpu.SemaphoreType.DMA((pushes,)),
            pltpu.SemaphoreType.DMA((2, rows, ny)),
            pltpu.SemaphoreType.DMA((2, rows, ny)),
        ],
        compiler_params=pltpu.CompilerParams(collective_id=2, has_side_effects=True),
    )(shard)


def fused_kernel(nz, nx, tasks, shard_ref, count_ref, occ_ref, ti_ref, tj_ref, vir_ref, out_ref, dens_ref,
                 mine, rows_ref, cols_ref, flip, vsum, amp, total, stage, xmsg, ymsg, keep, fold, part, gath, strip, plane,
                 row_sem, col_sem, x_sem, y_sem, keep_sem, fold_sem, part_sem, plane_sem, line_sem, dens_sem,
                 first_send, relay_send, pass_send, gamma_send, fold_send, part_send, plane_send, col_send, dens_send, home_sem):
    virtuals, aux = flip.shape
    row, col = lax.axis_index("orow"), lax.axis_index("ocol")
    z, x, y, k = row // nx, lax.rem(row, nx), col // 2, lax.rem(col, 2)
    nx_, ny_, nk_ = 1 - x, 1 - y, 1 - k
    parity = lax.rem(z, 2)
    twin, mirror = z + 1 - 2 * parity, nz - 1 - z
    owner = parity == k
    other = jnp.logical_not(owner)
    both = jnp.logical_and
    dif = lax.rem(parity + k, 2)
    block = (z - parity + k) * nx + x
    cores = (k, nk_)

    def device(dz, dx, dy, dk):
        return {"orow": dz * nx + dx, "ocol": dy * 2 + dk}

    def remote(src, dst, send, take, where):
        return pltpu.make_async_remote_copy(
            src_ref=src, dst_ref=dst, send_sem=send, recv_sem=take, device_id=where, device_id_type=MESH)

    sibling = device(z, x, y, nk_)

    def arrive(ref, sem):
        remote(ref, ref, first_send.at[0], sem, sibling).wait_recv()

    barrier = pltpu.get_barrier_semaphore()
    peers = [sibling, device(nz - 1 - twin, x, y, k)]
    peers += [device(dz, x, ny_, k) for dz in (twin, mirror, nz - 1 - twin)]
    for c in range(2):
        peers += [device(z, x, ny_, c), device(z, nx_, y, c), device(twin, x, y, c), device(mirror, x, y, c)]
    for peer in peers:
        pl.semaphore_signal(barrier, inc=1, device_id=peer, device_id_type=MESH)

    count = count_ref[row]
    for r in range(2):
        o = lax.rem(y + r, 2)
        active = jnp.where(count > o, 1.0, 0.0).astype(jnp.float32)
        mine[r] = (shard_ref[o].astype(jnp.float32) * active).astype(jnp.bfloat16)
    cols_ref[0, 0] = mine[0]

    @pl.when(owner)
    def _():
        for r in range(2):
            rows_ref[r, 0] = mine[r]

    pl.semaphore_wait(barrier, len(peers))

    def give_row(source, r, q, where, slot):
        return remote(mine.at[source], rows_ref.at[r, q], first_send.at[slot], row_sem.at[r, q], where)

    def give_col(zr, q, where, slot):
        return remote(mine.at[0], cols_ref.at[zr, q], first_send.at[slot], col_sem.at[zr, q], where)

    opening = [
        give_col(2, 0, device(mirror, x, y, k), 3),
        give_row(1, 0, 2 + dif, device(z, x, ny_, parity), 0),
        give_col(1, 0, device(z, nx_, y, k), 2),
        give_row(0, 1, 2 + dif, device(z, x, ny_, parity), 5),
        give_row(1, 1, dif, device(twin, x, y, parity), 6),
        give_row(0, 0, dif, device(twin, x, y, parity), 1),
        give_col(0, 1, sibling, 4),
    ]
    home = [give_row(0, 0, 1, sibling, 7), give_row(1, 1, 1, sibling, 8)]
    for copy in opening:
        copy.start()

    @pl.when(other)
    def _():
        for copy in home:
            copy.start()

    def wait_row(r, q):
        arrive(rows_ref.at[r, q], row_sem.at[r, q])

    def wait_col(zr, q):
        arrive(cols_ref.at[zr, q], col_sem.at[zr, q])

    def relays(c):
        source = rows_ref.at[0, 2 + c]
        return [
            remote(source, cols_ref.at[2, 2], relay_send.at[c, 1], col_sem.at[2, 2], device(mirror, x, y, cores[c])),
            remote(source, cols_ref.at[1, 2], relay_send.at[c, 0], col_sem.at[1, 2], device(z, nx_, y, cores[c])),
            remote(source, cols_ref.at[0, 3 - c], relay_send.at[c, 3], col_sem.at[0, 3 - c], sibling),
        ]

    def at_home(c):
        return pltpu.make_async_copy(rows_ref.at[0, 2 + c], cols_ref.at[0, 2 + c], home_sem.at[c])

    def across(r, c):
        return remote(rows_ref.at[r, c], rows_ref.at[1 - r, 2 + c], relay_send.at[c, r], row_sem.at[1 - r, 2 + c],
                      device(z, x, ny_, k))

    @pl.when(owner)
    def _():
        for c in range(2):
            wait_row(0, 2 + c)
            for copy in relays(c):
                copy.start()
            at_home(c).start()

    @pl.when(other)
    def _():
        for r in (1, 0):
            for c in range(2):
                wait_row(r, c)
                across(r, c).start()

    places = (z * nx + x, z * nx + nx_, mirror * nx + x, mirror * nx + nx_)

    def tally(t, carry):
        a, b = ti_ref[t], tj_ref[t]
        result = []
        for zr, j in enumerate(places):
            ahead = jnp.where(a == block, 1, 0) * jnp.where(b == j, 1, 0)
            behind = jnp.where(b == block, 1, 0) * jnp.where(a == j, 1, 0)
            result += [carry[2 * zr] + ahead, carry[2 * zr + 1] + behind]
        return tuple(result)

    tallies = lax.fori_loop(0, tasks, tally, (jnp.int32(0),) * (2 * nz))
    ahead = [tallies[2 * zr].astype(jnp.float32) for zr in range(nz)]
    weight = [(tallies[2 * zr] + tallies[2 * zr + 1]).astype(jnp.float32) for zr in range(nz)]
    spread = jnp.broadcast_to(vir_ref[...].reshape(1, virtuals), vsum.shape)
    vsum[...] = spread + spread.T

    def pass_on(zr, a, slot):
        q = 2 * a
        return remote(cols_ref.at[zr, q], cols_ref.at[zr, q + 1], pass_send.at[slot], col_sem.at[zr, q + 1], sibling)

    passed = []

    def launch(copy):
        copy.start()
        passed.append(copy)

    def take(zr, a):
        q = 2 * a
        wait_col(zr, q)
        if zr == 2:
            launch(remote(cols_ref.at[2, q], cols_ref.at[3, q], pass_send.at[len(passed)], col_sem.at[3, q],
                          device(z, nx_, y, k)))
        launch(pass_on(zr, a, len(passed)))

    def amplitudes(r, zr):
        kij = jnp.dot(flip[...], cols_ref[zr].reshape(aux, virtuals), preferred_element_type=jnp.float32)
        pair = occ_ref[block * 2 + lax.rem(y + r, 2)] + occ_ref[places[zr] * 2 + y]
        amp[zr, r] = ((2.0 * kij - kij.T) / (pair - vsum[...])).astype(jnp.bfloat16)

    take(1, 0)
    take(2, 0)
    take(1, 1)
    take(2, 1)

    @pl.when(owner)
    def _():
        wait_row(0, 1)

    @pl.when(other)
    def _():
        for c in range(2):
            wait_row(0, 2 + c)

    flip[...] = rows_ref[0].reshape(aux, virtuals).T
    wait_col(0, 1)

    @pl.when(owner)
    def _():
        for c in range(2):
            at_home(c).wait()

    @pl.when(other)
    def _():
        for c in range(2):
            wait_col(0, 2 + c)

    amplitudes(0, 0)
    for q in (1, 3):
        wait_col(1, q)
    amplitudes(0, 1)
    take(3, 0)
    for q in (1, 3):
        wait_col(2, q)
    amplitudes(0, 2)
    take(3, 1)
    for q in (1, 3):
        wait_col(3, q)
    amplitudes(0, 3)

    def gamma_sends(r, a, c):
        over_z, over_y = k == c, k == 1 - c
        q = 2 * a + c
        src, send = stage.at[r, q], gamma_send.at[r, q]
        if a == 0:
            sends = [(both(other, over_z), remote(src, xmsg.at[r], send, x_sem.at[r], device(twin, x, y, cores[c])))]
            if c == 1:
                sends.append((owner, remote(total.at[r, q], keep.at[r], send, keep_sem.at[r], sibling)))
            return sends
        return [
            (both(other, over_z), remote(src, fold.at[r], send, fold_sem.at[r], device(twin, x, y, k))),
            (both(other, over_y), remote(src, fold.at[1 - r], send, fold_sem.at[1 - r], device(z, x, ny_, k))),
            (both(owner, over_y), remote(src, ymsg.at[1 - r], send, y_sem.at[1 - r], device(z, x, ny_, cores[c]))),
        ]

    def guarded(condition, action):
        @pl.when(condition)
        def _():
            action()

    def send_off(r, a, c):
        for condition, copy in gamma_sends(r, a, c):
            guarded(condition, copy.start)

    def gamma(r, a, hold=False):
        for c in range(2):
            q = 2 * a + c
            value = weight[0] * lax.dot_general(
                cols_ref[0, q], amp[0, r], (((1,), (1,)), ((), ())), preferred_element_type=jnp.float32)
            for zr in range(1, nz):
                value += weight[zr] * lax.dot_general(
                    cols_ref[zr, q], amp[zr, r], (((1,), (1,)), ((), ())), preferred_element_type=jnp.float32)
            total[r, q] = value
            stage[r, q] = value.astype(jnp.bfloat16)
            if q == 0:
                @pl.when(owner)
                def _():
                    keep[r] = value

            if not hold:
                send_off(r, a, c)

    def folded(own, r, c):
        if own:
            return remote(stage.at[r, 2 + c], ymsg.at[1 - r], fold_send.at[r], y_sem.at[1 - r], device(z, x, ny_, cores[c]))
        return remote(stage.at[r, c], xmsg.at[r], fold_send.at[r], x_sem.at[r], device(twin, x, y, cores[c]))

    def holders(own):
        return [(c, both(owner, k == c) if own else both(other, k == 1 - c)) for c in range(2)]

    def fold_in(own, r):
        for c, condition in holders(own):
            @pl.when(condition)
            def _():
                arrive(fold.at[r], fold_sem.at[r])
                q = (2 if own else 0) + c
                stage[r, q] = (total[r, q] + fold[r].astype(jnp.float32)).astype(jnp.bfloat16)
                folded(own, r, c).start()

    gamma(0, 1)

    @pl.when(owner)
    def _():
        for q in (1, 2, 3):
            wait_row(1, q)

    @pl.when(other)
    def _():
        for q in (2, 3):
            wait_row(1, q)

    flip[...] = rows_ref[1].reshape(aux, virtuals).T
    for zr in range(nz):
        amplitudes(1, zr)

    def square(zr):
        return sum(lax.dot_general(amp[zr, r], amp[zr, r], (((1,), (1,)), ((), ())),
                                   preferred_element_type=jnp.float32) for r in range(2))

    dens = ahead[0] * square(0)
    for zr in range(1, nz):
        dens += ahead[zr] * square(zr)
    part[...] = dens.reshape(part.shape)
    me = x * 2 + k
    quad = []
    for dx in range(2):
        for dk in range(2):
            if dx or dk:
                tx, tk = lax.rem(x + dx, 2), lax.rem(k + dk, 2)
                quad.append((dx * 2 + dk, tx * 2 + tk, device(z, tx, y, tk)))
    line = []
    for slot, dz in enumerate((z, twin, mirror, nz - 1 - twin)):
        for dy in range(2):
            if slot or dy:
                line.append((slot * 2 + dy, dz, device(dz, x, lax.rem(y + dy, 2), k)))

    def scatter(slot, there, where):
        return remote(part.at[there], gath.at[slot], part_send.at[slot - 1], part_sem.at[slot], where)

    def swap(slot, dz, where):
        return remote(strip.at[dz], plane.at[slot], plane_send.at[slot - 1], plane_sem.at[slot], where)

    def collect(slot, dz, where):
        return remote(dens_ref.at[me, z], dens_ref.at[me, z], col_send.at[slot // 2 - 1], line_sem.at[z], where)

    def spread_out(slot, there, where):
        return remote(dens_ref.at[me], dens_ref.at[me], dens_send.at[slot - 1], dens_sem.at[me], where)

    for item in quad:
        scatter(*item).start()
    gath[0] = part[me]
    gamma(0, 0, True)
    for slot, there, where in quad:
        arrive(gath.at[slot], part_sem.at[slot])
    strip[...] = (gath[0] + gath[1]) + (gath[2] + gath[3])
    for item in line:
        swap(*item).start()
    plane[0] = strip[z]
    for c in range(2):
        send_off(0, 0, c)
    fold_in(True, 0)
    gamma(1, 1)
    for slot, dz, where in line:
        arrive(plane.at[slot], plane_sem.at[slot])
    dens_ref[me, z] = (((plane[0] + plane[1]) + (plane[2] + plane[3]))
                       + ((plane[4] + plane[5]) + (plane[6] + plane[7]))) * (1.0 / tasks)
    for item in line:
        if item[0] % 2 == 0:
            collect(*item).start()
    gamma(1, 0)
    fold_in(False, 1)
    fold_in(True, 1)
    fold_in(False, 0)
    for slot, dz, where in line:
        if slot % 2 == 0:
            arrive(dens_ref.at[me, dz], line_sem.at[dz])
    for item in quad:
        spread_out(*item).start()

    for r in range(2):
        guarded(other, lambda: arrive(keep.at[r], keep_sem.at[r]))
        arrive(xmsg.at[r], x_sem.at[r])
        arrive(ymsg.at[r], y_sem.at[r])
    for o in range(2):
        r = lax.rem(y + o, 2)
        out_ref[:, o, :] = (keep[r] + xmsg[r].astype(jnp.float32)) + ymsg[r].astype(jnp.float32)

    for slot, there, where in quad:
        arrive(dens_ref.at[there], dens_sem.at[there])
    for copy in opening + passed:
        copy.wait_send()

    @pl.when(other)
    def _():
        for copy in home:
            copy.wait_send()
        for r in range(2):
            for c in range(2):
                across(r, c).wait_send()

    @pl.when(owner)
    def _():
        for c in range(2):
            for copy in relays(c):
                copy.wait_send()

    for r in range(2):
        for a in range(2):
            for c in range(2):
                for condition, copy in gamma_sends(r, a, c):
                    guarded(condition, copy.wait_send)
    for own in (True, False):
        for c, condition in holders(own):
            for r in range(2):
                guarded(condition, folded(own, r, c).wait_send)
    for item in quad:
        scatter(*item).wait_send()
        spread_out(*item).wait_send()
    for item in line:
        swap(*item).wait_send()
        if item[0] % 2 == 0:
            collect(*item).wait_send()


def fused(integrals, occ_count, occ_energy, vir_energy, task_iblock, task_jblock, nz, nx):
    aux_local, orbitals, virtuals = integrals.shape
    aux = aux_local * lax.axis_size("ocol")
    tasks = task_jblock.shape[0]
    share = virtuals // (4 * nz)
    half, full = jnp.bfloat16, jnp.float32
    dma = pltpu.SemaphoreType.DMA
    vmem, smem = pl.BlockSpec(memory_space=pltpu.VMEM), pl.BlockSpec(memory_space=pltpu.SMEM)
    out, dens = pl.pallas_call(
        functools.partial(fused_kernel, nz, nx, tasks),
        out_shape=[
            jax.ShapeDtypeStruct((aux_local, orbitals, virtuals), full),
            jax.ShapeDtypeStruct((4, nz, share, virtuals), full),
        ],
        in_specs=[vmem, smem, smem, smem, smem, vmem],
        out_specs=[vmem, vmem],
        scratch_shapes=[
            pltpu.VMEM((2, aux_local, virtuals), half),
            pltpu.VMEM((2, 4, aux_local, virtuals), half),
            pltpu.VMEM((nz, 4, aux_local, virtuals), half),
            pltpu.VMEM((virtuals, aux), half),
            pltpu.VMEM((virtuals, virtuals), full),
            pltpu.VMEM((nz, 2, virtuals, virtuals), half),
            pltpu.VMEM((2, 4, aux_local, virtuals), full),
            pltpu.VMEM((2, 4, aux_local, virtuals), half),
            pltpu.VMEM((2, aux_local, virtuals), half),
            pltpu.VMEM((2, aux_local, virtuals), half),
            pltpu.VMEM((2, aux_local, virtuals), full),
            pltpu.VMEM((2, aux_local, virtuals), half),
            pltpu.VMEM((4, nz, share, virtuals), full),
            pltpu.VMEM((4, nz, share, virtuals), full),
            pltpu.VMEM((nz, share, virtuals), full),
            pltpu.VMEM((2 * nz, share, virtuals), full),
            dma((2, 4)), dma((nz, 4)), dma((2,)), dma((2,)), dma((2,)), dma((2,)), dma((4,)), dma((2 * nz,)), dma((nz,)), dma((4,)),
            dma((9,)), dma((2, 4)), dma((8,)), dma((2, 4)), dma((2,)), dma((3,)), dma((2 * nz - 1,)), dma((nz - 1,)), dma((3,)), dma((2,)),
        ],
        compiler_params=pltpu.CompilerParams(
            collective_id=3, has_side_effects=True, vmem_limit_bytes=56 * 1024 * 1024),
    )(jnp.transpose(integrals, (1, 0, 2)), occ_count, occ_energy, task_iblock[:, 0], task_jblock, vir_energy)
    return out, dens.reshape(virtuals, virtuals)


def local(integrals, occ_count, occ_energy, vir_energy, task_iblock, task_jblock):
    aux_local, orbitals, virtuals = integrals.shape
    span = orbitals * virtuals
    blocks = lax.axis_size("orow")
    cols = lax.axis_size("ocol")
    if blocks == 8 and cols == 4 and orbitals == 2:
        return fused(integrals, occ_count, occ_energy, vir_energy, task_iblock, task_jblock, blocks // 2, 2)
    row = lax.axis_index("orow")
    col = lax.axis_index("ocol")
    aux = aux_local * cols
    active = jnp.arange(orbitals) < occ_count[row]
    masked = integrals * active.astype(jnp.bfloat16)[None, :, None]
    shard = masked.reshape(aux_local, span)
    gathered = gather_all(shard).reshape(blocks, aux, span)
    i_list, j_list = task_iblock[:, 0], task_jblock
    ids = jnp.arange(blocks)
    i_hot = i_list[None, :] == ids[:, None]
    j_hot = j_list[None, :] == ids[:, None]
    first = jnp.sum((i_list == row)[None, :] & j_hot, axis=1).astype(jnp.int32)
    second = jnp.sum((j_list == row)[None, :] & i_hot, axis=1).astype(jnp.int32)
    numbers = jnp.concatenate([jnp.stack([row, col]).astype(jnp.int32), first + second, first])
    gamma, dens = pl.pallas_call(
        functools.partial(pair_kernel, orbitals, cols),
        grid_spec=pltpu.PrefetchScalarGridSpec(
            num_scalar_prefetch=2,
            grid=(blocks,),
            in_specs=[
                pl.BlockSpec((1, aux, span), lambda s, num, occ: (num[0], 0, 0)),
                pl.BlockSpec((1, aux, span), lambda s, num, occ: (s, 0, 0)),
                pl.BlockSpec((1, aux_local, span), lambda s, num, occ: (s, num[1], 0)),
                pl.BlockSpec((1, virtuals), lambda s, num, occ: (0, 0)),
                pl.BlockSpec((virtuals, 1), lambda s, num, occ: (0, 0)),
            ],
            out_specs=[
                pl.BlockSpec((aux_local, span), lambda s, num, occ: (0, 0)),
                pl.BlockSpec((virtuals // cols, virtuals), lambda s, num, occ: (0, 0)),
            ],
            scratch_shapes=[pltpu.VMEM((span, aux), jnp.bfloat16), pltpu.VMEM((orbitals, virtuals, span), jnp.bfloat16)],
        ),
        out_shape=[
            jax.ShapeDtypeStruct((aux_local, span), jnp.float32),
            jax.ShapeDtypeStruct((virtuals // cols, virtuals), jnp.float32),
        ],
        compiler_params=pltpu.CompilerParams(vmem_limit_bytes=56 * 1024 * 1024),
    )(numbers, occ_energy, gathered, gathered, gathered, vir_energy[None, :], vir_energy[:, None])
    density = sum_density(dens, i_list.shape[0])
    return gamma.reshape(aux_local, orbitals, virtuals), density


def solution(mesh):
    return jax.shard_map(
        local,
        mesh=mesh,
        in_specs=(P("ocol", "orow", None), P(), P(), P(), P(), P()),
        out_specs=(P("ocol", "orow", None), P()),
        check_vma=False,
    )
```

```python
import functools

import jax
import jax.numpy as jnp
from jax import lax
from jax.experimental import pallas as pl
from jax.experimental.pallas import tpu as pltpu
from jax.sharding import PartitionSpec as P

MESH = pl.DeviceIdType.MESH


def pair_kernel(orbitals, cols, num_ref, occ_ref, gr_ref, gs_ref, gc_ref, vrow_ref, vcol_ref, gamma_ref, dens_ref, flip_ref, amp_ref):
    s = pl.program_id(0)
    blocks = pl.num_programs(0)
    row, col = num_ref[0], num_ref[1]
    virtuals = vrow_ref.shape[1]

    @pl.when(s == 0)
    def _():
        gamma_ref[...] = jnp.zeros_like(gamma_ref)
        dens_ref[...] = jnp.zeros_like(dens_ref)
        flip_ref[...] = gr_ref[0].T

    touch = num_ref[2 + s]
    first = num_ref[2 + blocks + s]

    @pl.when(touch > 0)
    def _():
        weight = touch.astype(jnp.float32)
        for i in range(orbitals):
            own = pl.ds(i * virtuals, virtuals)
            k_rows = jnp.dot(flip_ref[own, :], gs_ref[0], preferred_element_type=jnp.float32)
            parts = []
            for j in range(orbitals):
                k_ij = k_rows[:, j * virtuals:(j + 1) * virtuals]
                pair = occ_ref[row * orbitals + i] + occ_ref[s * orbitals + j]
                denominator = (pair - vcol_ref[...]) - vrow_ref[...]
                parts.append(((2.0 * k_ij - k_ij.T) / denominator).astype(jnp.bfloat16))
            amp = jnp.concatenate(parts, axis=1)
            amp_ref[i] = amp
            gamma_ref[:, own] += weight * lax.dot_general(
                gc_ref[0], amp, (((1,), (1,)), ((), ())), preferred_element_type=jnp.float32)

        @pl.when(first > 0)
        def _():
            strip = virtuals // cols
            count = first.astype(jnp.float32)
            for i in range(orbitals):
                mine = amp_ref[i, pl.ds(pl.multiple_of(col * strip, strip), strip), :]
                dens_ref[...] += count * lax.dot_general(
                    mine, amp_ref[i], (((1,), (1,)), ((), ())), preferred_element_type=jnp.float32)


def density_kernel(scale, part_ref, out_ref, arrived, send_sem, take_sem, pass_sem, row_sem, fan_sem, col_sem):
    rows, cols = lax.axis_size("orow"), lax.axis_size("ocol")
    row, col = lax.axis_index("orow"), lax.axis_index("ocol")
    barrier = pltpu.get_barrier_semaphore()

    def peer(step):
        return lax.rem(row + step, rows)

    def other(step):
        return lax.rem(col + step, cols)

    @pl.loop(1, rows)
    def _(step):
        pl.semaphore_signal(barrier, inc=1, device_id={"orow": peer(step)}, device_id_type=MESH)

    @pl.loop(1, cols)
    def _(step):
        pl.semaphore_signal(barrier, inc=1, device_id={"ocol": other(step)}, device_id_type=MESH)

    pl.semaphore_wait(barrier, rows + cols - 2)

    def scatter(step):
        return pltpu.make_async_remote_copy(
            src_ref=part_ref.at[peer(step)], dst_ref=arrived.at[step - 1], send_sem=send_sem.at[step - 1],
            recv_sem=take_sem.at[step - 1], device_id={"orow": peer(step)}, device_id_type=MESH)

    def spread(step):
        spot = out_ref.at[col, row]
        return pltpu.make_async_remote_copy(
            src_ref=spot, dst_ref=spot, send_sem=pass_sem.at[step - 1],
            recv_sem=row_sem.at[step - 1], device_id={"orow": peer(step)}, device_id_type=MESH)

    def fan(step):
        spot = out_ref.at[col]
        return pltpu.make_async_remote_copy(
            src_ref=spot, dst_ref=spot, send_sem=fan_sem.at[step - 1],
            recv_sem=col_sem.at[step - 1], device_id={"ocol": other(step)}, device_id_type=MESH)

    @pl.loop(1, rows)
    def _(step):
        scatter(step).start()

    total = part_ref[row]
    for step in range(1, rows):
        scatter(step).wait()
        total = total + arrived[step - 1]
    out_ref[col, row] = total * scale

    @pl.loop(1, rows)
    def _(step):
        spread(step).start()

    @pl.loop(1, rows)
    def _(step):
        spread(step).wait()

    @pl.loop(1, cols)
    def _(step):
        fan(step).start()

    @pl.loop(1, cols)
    def _(step):
        fan(step).wait()


def sum_density(part, tasks):
    rows, cols = lax.axis_size("orow"), lax.axis_size("ocol")
    strip, virtuals = part.shape
    share = strip // rows
    full = pl.pallas_call(
        functools.partial(density_kernel, 1.0 / tasks),
        out_shape=jax.ShapeDtypeStruct((cols, rows, share, virtuals), jnp.float32),
        in_specs=[pl.BlockSpec(memory_space=pltpu.VMEM)],
        out_specs=pl.BlockSpec(memory_space=pltpu.VMEM),
        scratch_shapes=[
            pltpu.VMEM((rows - 1, share, virtuals), jnp.float32),
            pltpu.SemaphoreType.DMA((rows - 1,)),
            pltpu.SemaphoreType.DMA((rows - 1,)),
            pltpu.SemaphoreType.DMA((rows - 1,)),
            pltpu.SemaphoreType.DMA((rows - 1,)),
            pltpu.SemaphoreType.DMA((cols - 1,)),
            pltpu.SemaphoreType.DMA((cols - 1,)),
        ],
        compiler_params=pltpu.CompilerParams(collective_id=1, has_side_effects=True),
    )(part.reshape(rows, share, virtuals))
    return full.reshape(virtuals, virtuals)


def gather_kernel(nz, nx, ny, cut, shard_ref, all_ref, own_sem, send_sem, line_sem, pair_sem):
    aux_local = shard_ref.shape[0]
    row, col = lax.axis_index("orow"), lax.axis_index("ocol")
    z, x, y, k = row // nx, lax.rem(row, nx), col // 2, lax.rem(col, 2)
    spans = (pl.ds(0, cut), pl.ds(cut, aux_local - cut))

    def turn(at, by, extent):
        return lax.rem(at + by, extent)

    def place(dz=0, dx=0, dy=0):
        return turn(z, dz, nz) * nx + turn(x, dx, nx), turn(y, dy, ny)

    def device(dz=0, dx=0, dy=0, dk=0):
        r, c = place(dz, dx, dy)
        return {"orow": r, "ocol": c * 2 + lax.rem(k + dk, 2)}

    near = sorted(range(1, nz), key=lambda d: min(d, nz - d))
    lines = {
        "z": [dict(dz=d) for d in near],
        "x": [dict(dx=d) for d in range(1, nx)],
        "y": [dict(dy=d) for d in range(1, ny)],
    }
    peers = lines["z"] + lines["x"] + lines["y"] + [dict(dk=1)]
    barrier = pltpu.get_barrier_semaphore()
    for peer in peers:
        pl.semaphore_signal(barrier, inc=1, device_id=device(**peer), device_id_type=MESH)
    pl.semaphore_wait(barrier, len(peers))

    sent = []

    def push(piece, at, source, sem, peer):
        r, c = place(**at)
        copy = pltpu.make_async_remote_copy(
            src_ref=source, dst_ref=all_ref.at[r, c * 2 + k, spans[piece]], send_sem=send_sem.at[len(sent)],
            recv_sem=sem, device_id=device(**peer), device_id_type=MESH)
        copy.start()
        sent.append(copy)

    def pass_on(piece, at, order):
        r, c = place(**at)
        own = not at
        source = shard_ref.at[spans[piece]] if own else all_ref.at[r, c * 2 + k, spans[piece]]
        for axis in order:
            for peer in lines[axis]:
                push(piece, at, source, line_sem.at[piece, r, c], peer)
        push(piece, at, source, pair_sem.at[piece, r, c], dict(dk=1))

    def take(piece, at, sem, core):
        r, c = place(**at)
        spot = all_ref.at[r, c * 2 + core, spans[piece]]
        pltpu.make_async_remote_copy(
            src_ref=spot, dst_ref=spot, send_sem=send_sem.at[0], recv_sem=sem.at[piece, r, c],
            device_id=device(dk=1), device_id_type=MESH).wait_recv()

    def relay(piece, at, order):
        take(piece, at, line_sem, k)
        pass_on(piece, at, order)

    keep = pltpu.make_async_copy(shard_ref, all_ref.at[row, col], own_sem)
    keep.start()
    pass_on(1, {}, "yzx")
    pass_on(0, {}, "zxy")
    for side in lines["y"]:
        relay(1, side, "zx")
    for up in lines["z"]:
        relay(0, up, "xy")
    for up in [{}] + lines["z"]:
        for across in lines["x"]:
            relay(0, up | across, "y")
        if up:
            for side in [{}] + lines["y"]:
                relay(1, up | side, "x")
    for up in [{}] + lines["z"]:
        for across in [{}] + lines["x"]:
            for side in lines["y"]:
                relay(0, up | across | side, "")
        for side in [{}] + lines["y"]:
            for across in lines["x"]:
                relay(1, up | across | side, "")
    for dz in range(nz):
        for dx in range(nx):
            for dy in range(ny):
                for piece in (0, 1):
                    take(piece, dict(dz=dz, dx=dx, dy=dy), pair_sem, 1 - k)
    keep.wait()
    for copy in sent:
        copy.wait_send()


def gather_all(shard):
    rows, cols = lax.axis_size("orow"), lax.axis_size("ocol")
    ny = cols // 2
    nx = ny if rows % ny == 0 else 1
    nz = rows // nx
    aux_local, span = shard.shape
    cut = aux_local * 7 // 11 // 16 * 16
    pushes = 2 * nz * nx * ny + (nz - 1) + nz * (nx - 1) + nz * nx * (ny - 1) + (ny - 1) + ny * (nz - 1) + nz * ny * (nx - 1)
    return pl.pallas_call(
        functools.partial(gather_kernel, nz, nx, ny, cut),
        out_shape=jax.ShapeDtypeStruct((rows, cols, aux_local, span), shard.dtype),
        in_specs=[pl.BlockSpec(memory_space=pltpu.VMEM)],
        out_specs=pl.BlockSpec(memory_space=pl.ANY),
        scratch_shapes=[
            pltpu.SemaphoreType.DMA,
            pltpu.SemaphoreType.DMA((pushes,)),
            pltpu.SemaphoreType.DMA((2, rows, ny)),
            pltpu.SemaphoreType.DMA((2, rows, ny)),
        ],
        compiler_params=pltpu.CompilerParams(collective_id=2, has_side_effects=True),
    )(shard)


def fused_kernel(nz, nx, tasks, shard_ref, count_ref, occ_ref, ti_ref, tj_ref, vir_ref, out_ref, dens_ref,
                 mine, rows_ref, cols_ref, flip, vsum, amp, total, stage, xmsg, ymsg, keep, fold, part, gath, strip, plane,
                 row_sem, col_sem, x_sem, y_sem, keep_sem, fold_sem, part_sem, plane_sem, line_sem, dens_sem,
                 first_send, relay_send, pass_send, gamma_send, fold_send, part_send, plane_send, col_send, dens_send, home_sem):
    virtuals, aux = flip.shape
    row, col = lax.axis_index("orow"), lax.axis_index("ocol")
    z, x, y, k = row // nx, lax.rem(row, nx), col // 2, lax.rem(col, 2)
    nx_, ny_, nk_ = 1 - x, 1 - y, 1 - k
    parity = lax.rem(z, 2)
    twin, mirror = z + 1 - 2 * parity, nz - 1 - z
    owner = parity == k
    other = jnp.logical_not(owner)
    both = jnp.logical_and
    dif = lax.rem(parity + k, 2)
    block = (z - parity + k) * nx + x
    cores = (k, nk_)

    def device(dz, dx, dy, dk):
        return {"orow": dz * nx + dx, "ocol": dy * 2 + dk}

    def remote(src, dst, send, take, where):
        return pltpu.make_async_remote_copy(
            src_ref=src, dst_ref=dst, send_sem=send, recv_sem=take, device_id=where, device_id_type=MESH)

    sibling = device(z, x, y, nk_)

    def arrive(ref, sem):
        remote(ref, ref, first_send.at[0], sem, sibling).wait_recv()

    barrier = pltpu.get_barrier_semaphore()
    peers = [sibling, device(nz - 1 - twin, x, y, k)]
    for c in range(2):
        peers += [device(z, x, ny_, c), device(z, nx_, y, c), device(twin, x, y, c), device(mirror, x, y, c)]
    for peer in peers:
        pl.semaphore_signal(barrier, inc=1, device_id=peer, device_id_type=MESH)

    count = count_ref[row]
    for r in range(2):
        o = lax.rem(y + r, 2)
        active = jnp.where(count > o, 1.0, 0.0).astype(jnp.float32)
        mine[r] = (shard_ref[o].astype(jnp.float32) * active).astype(jnp.bfloat16)
    cols_ref[0, 0] = mine[0]

    @pl.when(owner)
    def _():
        for r in range(2):
            rows_ref[r, 0] = mine[r]

    pl.semaphore_wait(barrier, len(peers))

    def give_row(source, r, q, where, slot):
        return remote(mine.at[source], rows_ref.at[r, q], first_send.at[slot], row_sem.at[r, q], where)

    def give_col(zr, q, where, slot):
        return remote(mine.at[0], cols_ref.at[zr, q], first_send.at[slot], col_sem.at[zr, q], where)

    opening = [
        give_col(2, 0, device(mirror, x, y, k), 3),
        give_row(1, 0, 2 + dif, device(z, x, ny_, parity), 0),
        give_col(1, 0, device(z, nx_, y, k), 2),
        give_row(0, 1, 2 + dif, device(z, x, ny_, parity), 5),
        give_row(1, 1, dif, device(twin, x, y, parity), 6),
        give_row(0, 0, dif, device(twin, x, y, parity), 1),
        give_col(0, 1, sibling, 4),
    ]
    home = [give_row(0, 0, 1, sibling, 7), give_row(1, 1, 1, sibling, 8)]
    for copy in opening:
        copy.start()

    @pl.when(other)
    def _():
        for copy in home:
            copy.start()

    def wait_row(r, q):
        arrive(rows_ref.at[r, q], row_sem.at[r, q])

    def wait_col(zr, q):
        arrive(cols_ref.at[zr, q], col_sem.at[zr, q])

    def relays(c):
        source = rows_ref.at[0, 2 + c]
        return [
            remote(source, cols_ref.at[2, 2], relay_send.at[c, 1], col_sem.at[2, 2], device(mirror, x, y, cores[c])),
            remote(source, cols_ref.at[1, 2], relay_send.at[c, 0], col_sem.at[1, 2], device(z, nx_, y, cores[c])),
            remote(source, cols_ref.at[0, 3 - c], relay_send.at[c, 3], col_sem.at[0, 3 - c], sibling),
        ]

    def at_home(c):
        return pltpu.make_async_copy(rows_ref.at[0, 2 + c], cols_ref.at[0, 2 + c], home_sem.at[c])

    def across(r, c):
        return remote(rows_ref.at[r, c], rows_ref.at[1 - r, 2 + c], relay_send.at[c, r], row_sem.at[1 - r, 2 + c],
                      device(z, x, ny_, k))

    @pl.when(owner)
    def _():
        for c in range(2):
            wait_row(0, 2 + c)
            for copy in relays(c):
                copy.start()
            at_home(c).start()

    @pl.when(other)
    def _():
        for r in (1, 0):
            for c in range(2):
                wait_row(r, c)
                across(r, c).start()

    places = (z * nx + x, z * nx + nx_, mirror * nx + x, mirror * nx + nx_)

    def tally(t, carry):
        a, b = ti_ref[t], tj_ref[t]
        result = []
        for zr, j in enumerate(places):
            ahead = jnp.where(a == block, 1, 0) * jnp.where(b == j, 1, 0)
            behind = jnp.where(b == block, 1, 0) * jnp.where(a == j, 1, 0)
            result += [carry[2 * zr] + ahead, carry[2 * zr + 1] + behind]
        return tuple(result)

    tallies = lax.fori_loop(0, tasks, tally, (jnp.int32(0),) * (2 * nz))
    ahead = [tallies[2 * zr].astype(jnp.float32) for zr in range(nz)]
    weight = [(tallies[2 * zr] + tallies[2 * zr + 1]).astype(jnp.float32) for zr in range(nz)]
    spread = jnp.broadcast_to(vir_ref[...].reshape(1, virtuals), vsum.shape)
    vsum[...] = spread + spread.T

    def pass_on(zr, a, slot):
        q = 2 * a
        return remote(cols_ref.at[zr, q], cols_ref.at[zr, q + 1], pass_send.at[slot], col_sem.at[zr, q + 1], sibling)

    passed = []

    def launch(copy):
        copy.start()
        passed.append(copy)

    def take(zr, a):
        q = 2 * a
        wait_col(zr, q)
        if zr == 2:
            launch(remote(cols_ref.at[2, q], cols_ref.at[3, q], pass_send.at[len(passed)], col_sem.at[3, q],
                          device(z, nx_, y, k)))
        launch(pass_on(zr, a, len(passed)))

    def amplitudes(r, zr):
        kij = jnp.dot(flip[...], cols_ref[zr].reshape(aux, virtuals), preferred_element_type=jnp.float32)
        pair = occ_ref[block * 2 + lax.rem(y + r, 2)] + occ_ref[places[zr] * 2 + y]
        amp[zr, r] = ((2.0 * kij - kij.T) / (pair - vsum[...])).astype(jnp.bfloat16)

    take(1, 0)
    take(2, 0)
    take(1, 1)
    take(2, 1)

    @pl.when(owner)
    def _():
        wait_row(0, 1)

    @pl.when(other)
    def _():
        for c in range(2):
            wait_row(0, 2 + c)

    flip[...] = rows_ref[0].reshape(aux, virtuals).T
    wait_col(0, 1)

    @pl.when(owner)
    def _():
        for c in range(2):
            at_home(c).wait()

    @pl.when(other)
    def _():
        for c in range(2):
            wait_col(0, 2 + c)

    amplitudes(0, 0)
    for q in (1, 3):
        wait_col(1, q)
    amplitudes(0, 1)
    take(3, 0)
    for q in (1, 3):
        wait_col(2, q)
    amplitudes(0, 2)
    take(3, 1)
    for q in (1, 3):
        wait_col(3, q)
    amplitudes(0, 3)

    def gamma_sends(r, a, c):
        over_z, over_y = k == c, k == 1 - c
        q = 2 * a + c
        src, send = stage.at[r, q], gamma_send.at[r, q]
        if a == 0:
            sends = [(both(other, over_z), remote(src, xmsg.at[r], send, x_sem.at[r], device(twin, x, y, cores[c])))]
            if c == 1:
                sends.append((owner, remote(total.at[r, q], keep.at[r], send, keep_sem.at[r], sibling)))
            return sends
        return [
            (both(other, over_z), remote(src, fold.at[r], send, fold_sem.at[r], device(twin, x, y, k))),
            (both(other, over_y), remote(src, fold.at[1 - r], send, fold_sem.at[1 - r], device(z, x, ny_, k))),
            (both(owner, over_y), remote(src, ymsg.at[1 - r], send, y_sem.at[1 - r], device(z, x, ny_, cores[c]))),
        ]

    def guarded(condition, action):
        @pl.when(condition)
        def _():
            action()

    def send_off(r, a, c):
        for condition, copy in gamma_sends(r, a, c):
            guarded(condition, copy.start)

    def gamma(r, a, hold=False):
        for c in range(2):
            q = 2 * a + c
            value = weight[0] * lax.dot_general(
                cols_ref[0, q], amp[0, r], (((1,), (1,)), ((), ())), preferred_element_type=jnp.float32)
            for zr in range(1, nz):
                value += weight[zr] * lax.dot_general(
                    cols_ref[zr, q], amp[zr, r], (((1,), (1,)), ((), ())), preferred_element_type=jnp.float32)
            total[r, q] = value
            stage[r, q] = value.astype(jnp.bfloat16)
            if q == 0:
                @pl.when(owner)
                def _():
                    keep[r] = value

            if not hold:
                send_off(r, a, c)

    def folded(own, r, c):
        if own:
            return remote(stage.at[r, 2 + c], ymsg.at[1 - r], fold_send.at[r], y_sem.at[1 - r], device(z, x, ny_, cores[c]))
        return remote(stage.at[r, c], xmsg.at[r], fold_send.at[r], x_sem.at[r], device(twin, x, y, cores[c]))

    def holders(own):
        return [(c, both(owner, k == c) if own else both(other, k == 1 - c)) for c in range(2)]

    def fold_in(own, r):
        for c, condition in holders(own):
            @pl.when(condition)
            def _():
                arrive(fold.at[r], fold_sem.at[r])
                q = (2 if own else 0) + c
                stage[r, q] = (total[r, q] + fold[r].astype(jnp.float32)).astype(jnp.bfloat16)
                folded(own, r, c).start()

    gamma(0, 1)

    @pl.when(owner)
    def _():
        for q in (1, 2, 3):
            wait_row(1, q)

    @pl.when(other)
    def _():
        for q in (2, 3):
            wait_row(1, q)

    flip[...] = rows_ref[1].reshape(aux, virtuals).T
    for zr in range(nz):
        amplitudes(1, zr)

    gamma(1, 1)

    def square(zr):
        return sum(lax.dot_general(amp[zr, r], amp[zr, r], (((1,), (1,)), ((), ())),
                                   preferred_element_type=jnp.float32) for r in range(2))

    dens = ahead[0] * square(0)
    for zr in range(1, nz):
        dens += ahead[zr] * square(zr)
    part[...] = dens.reshape(part.shape)
    me = x * 2 + k
    quad = []
    for dx in range(2):
        for dk in range(2):
            if dx or dk:
                tx, tk = lax.rem(x + dx, 2), lax.rem(k + dk, 2)
                quad.append((dx * 2 + dk, tx * 2 + tk, device(z, tx, y, tk)))
    line = [(slot, dz, device(dz, x, y, k)) for slot, dz in ((1, twin), (2, mirror), (3, nz - 1 - twin))]
    pair = remote(plane.at[5], plane.at[4], plane_send.at[3], plane_sem.at[4], device(z, x, ny_, k))

    def scatter(slot, there, where):
        return remote(part.at[there], gath.at[slot], part_send.at[slot - 1], part_sem.at[slot], where)

    def swap(slot, dz, where):
        return remote(strip.at[dz], plane.at[slot], plane_send.at[slot - 1], plane_sem.at[slot], where)

    def collect(slot, dz, where):
        return remote(dens_ref.at[me, z], dens_ref.at[me, z], col_send.at[slot - 1], line_sem.at[z], where)

    def spread_out(slot, there, where):
        return remote(dens_ref.at[me], dens_ref.at[me], dens_send.at[slot - 1], dens_sem.at[me], where)

    for item in quad:
        scatter(*item).start()
    gath[0] = part[me]
    gamma(0, 0, True)
    for slot, there, where in quad:
        arrive(gath.at[slot], part_sem.at[slot])
    strip[...] = (gath[0] + gath[1]) + (gath[2] + gath[3])
    for item in line:
        swap(*item).start()
    plane[0] = strip[z]
    for c in range(2):
        send_off(0, 0, c)
    fold_in(True, 0)
    for slot, dz, where in line:
        arrive(plane.at[slot], plane_sem.at[slot])
    plane[5] = (plane[0] + plane[1]) + (plane[2] + plane[3])
    pair.start()
    gamma(1, 0)
    arrive(plane.at[4], plane_sem.at[4])
    dens_ref[me, z] = (plane[4] + plane[5]) * (1.0 / tasks)
    for item in line:
        collect(*item).start()
    fold_in(False, 1)
    fold_in(True, 1)
    fold_in(False, 0)
    for slot, dz, where in line:
        arrive(dens_ref.at[me, dz], line_sem.at[dz])
    for item in quad:
        spread_out(*item).start()

    for r in range(2):
        guarded(other, lambda: arrive(keep.at[r], keep_sem.at[r]))
        arrive(xmsg.at[r], x_sem.at[r])
        arrive(ymsg.at[r], y_sem.at[r])
    for o in range(2):
        r = lax.rem(y + o, 2)
        out_ref[:, o, :] = (keep[r] + xmsg[r].astype(jnp.float32)) + ymsg[r].astype(jnp.float32)

    for slot, there, where in quad:
        arrive(dens_ref.at[there], dens_sem.at[there])
    for copy in opening + passed:
        copy.wait_send()

    @pl.when(other)
    def _():
        for copy in home:
            copy.wait_send()
        for r in range(2):
            for c in range(2):
                across(r, c).wait_send()

    @pl.when(owner)
    def _():
        for c in range(2):
            for copy in relays(c):
                copy.wait_send()

    for r in range(2):
        for a in range(2):
            for c in range(2):
                for condition, copy in gamma_sends(r, a, c):
                    guarded(condition, copy.wait_send)
    for own in (True, False):
        for c, condition in holders(own):
            for r in range(2):
                guarded(condition, folded(own, r, c).wait_send)
    for item in quad:
        scatter(*item).wait_send()
        spread_out(*item).wait_send()
    for item in line:
        swap(*item).wait_send()
        collect(*item).wait_send()
    pair.wait_send()


def fused(integrals, occ_count, occ_energy, vir_energy, task_iblock, task_jblock, nz, nx):
    aux_local, orbitals, virtuals = integrals.shape
    aux = aux_local * lax.axis_size("ocol")
    tasks = task_jblock.shape[0]
    share = virtuals // (4 * nz)
    half, full = jnp.bfloat16, jnp.float32
    dma = pltpu.SemaphoreType.DMA
    vmem, smem = pl.BlockSpec(memory_space=pltpu.VMEM), pl.BlockSpec(memory_space=pltpu.SMEM)
    out, dens = pl.pallas_call(
        functools.partial(fused_kernel, nz, nx, tasks),
        out_shape=[
            jax.ShapeDtypeStruct((aux_local, orbitals, virtuals), full),
            jax.ShapeDtypeStruct((4, nz, share, virtuals), full),
        ],
        in_specs=[vmem, smem, smem, smem, smem, vmem],
        out_specs=[vmem, vmem],
        scratch_shapes=[
            pltpu.VMEM((2, aux_local, virtuals), half),
            pltpu.VMEM((2, 4, aux_local, virtuals), half),
            pltpu.VMEM((nz, 4, aux_local, virtuals), half),
            pltpu.VMEM((virtuals, aux), half),
            pltpu.VMEM((virtuals, virtuals), full),
            pltpu.VMEM((nz, 2, virtuals, virtuals), half),
            pltpu.VMEM((2, 4, aux_local, virtuals), full),
            pltpu.VMEM((2, 4, aux_local, virtuals), half),
            pltpu.VMEM((2, aux_local, virtuals), half),
            pltpu.VMEM((2, aux_local, virtuals), half),
            pltpu.VMEM((2, aux_local, virtuals), full),
            pltpu.VMEM((2, aux_local, virtuals), half),
            pltpu.VMEM((4, nz, share, virtuals), full),
            pltpu.VMEM((4, nz, share, virtuals), full),
            pltpu.VMEM((nz, share, virtuals), full),
            pltpu.VMEM((nz + 2, share, virtuals), full),
            dma((2, 4)), dma((nz, 4)), dma((2,)), dma((2,)), dma((2,)), dma((2,)), dma((4,)), dma((2 * nz,)), dma((nz,)), dma((4,)),
            dma((9,)), dma((2, 4)), dma((8,)), dma((2, 4)), dma((2,)), dma((3,)), dma((2 * nz - 1,)), dma((nz - 1,)), dma((3,)), dma((2,)),
        ],
        compiler_params=pltpu.CompilerParams(
            collective_id=3, has_side_effects=True, vmem_limit_bytes=56 * 1024 * 1024),
    )(jnp.transpose(integrals, (1, 0, 2)), occ_count, occ_energy, task_iblock[:, 0], task_jblock, vir_energy)
    return out, dens.reshape(virtuals, virtuals)


def local(integrals, occ_count, occ_energy, vir_energy, task_iblock, task_jblock):
    aux_local, orbitals, virtuals = integrals.shape
    span = orbitals * virtuals
    blocks = lax.axis_size("orow")
    cols = lax.axis_size("ocol")
    if blocks == 8 and cols == 4 and orbitals == 2:
        return fused(integrals, occ_count, occ_energy, vir_energy, task_iblock, task_jblock, blocks // 2, 2)
    row = lax.axis_index("orow")
    col = lax.axis_index("ocol")
    aux = aux_local * cols
    active = jnp.arange(orbitals) < occ_count[row]
    masked = integrals * active.astype(jnp.bfloat16)[None, :, None]
    shard = masked.reshape(aux_local, span)
    gathered = gather_all(shard).reshape(blocks, aux, span)
    i_list, j_list = task_iblock[:, 0], task_jblock
    ids = jnp.arange(blocks)
    i_hot = i_list[None, :] == ids[:, None]
    j_hot = j_list[None, :] == ids[:, None]
    first = jnp.sum((i_list == row)[None, :] & j_hot, axis=1).astype(jnp.int32)
    second = jnp.sum((j_list == row)[None, :] & i_hot, axis=1).astype(jnp.int32)
    numbers = jnp.concatenate([jnp.stack([row, col]).astype(jnp.int32), first + second, first])
    gamma, dens = pl.pallas_call(
        functools.partial(pair_kernel, orbitals, cols),
        grid_spec=pltpu.PrefetchScalarGridSpec(
            num_scalar_prefetch=2,
            grid=(blocks,),
            in_specs=[
                pl.BlockSpec((1, aux, span), lambda s, num, occ: (num[0], 0, 0)),
                pl.BlockSpec((1, aux, span), lambda s, num, occ: (s, 0, 0)),
                pl.BlockSpec((1, aux_local, span), lambda s, num, occ: (s, num[1], 0)),
                pl.BlockSpec((1, virtuals), lambda s, num, occ: (0, 0)),
                pl.BlockSpec((virtuals, 1), lambda s, num, occ: (0, 0)),
            ],
            out_specs=[
                pl.BlockSpec((aux_local, span), lambda s, num, occ: (0, 0)),
                pl.BlockSpec((virtuals // cols, virtuals), lambda s, num, occ: (0, 0)),
            ],
            scratch_shapes=[pltpu.VMEM((span, aux), jnp.bfloat16), pltpu.VMEM((orbitals, virtuals, span), jnp.bfloat16)],
        ),
        out_shape=[
            jax.ShapeDtypeStruct((aux_local, span), jnp.float32),
            jax.ShapeDtypeStruct((virtuals // cols, virtuals), jnp.float32),
        ],
        compiler_params=pltpu.CompilerParams(vmem_limit_bytes=56 * 1024 * 1024),
    )(numbers, occ_energy, gathered, gathered, gathered, vir_energy[None, :], vir_energy[:, None])
    density = sum_density(dens, i_list.shape[0])
    return gamma.reshape(aux_local, orbitals, virtuals), density


def solution(mesh):
    return jax.shard_map(
        local,
        mesh=mesh,
        in_specs=(P("ocol", "orow", None), P(), P(), P(), P(), P()),
        out_specs=(P("ocol", "orow", None), P()),
        check_vma=False,
    )
```

```python
import functools

import jax
import jax.numpy as jnp
from jax import lax
from jax.experimental import pallas as pl
from jax.experimental.pallas import tpu as pltpu
from jax.sharding import PartitionSpec as P

MESH = pl.DeviceIdType.MESH


def pair_kernel(orbitals, cols, num_ref, occ_ref, gr_ref, gs_ref, gc_ref, vrow_ref, vcol_ref, gamma_ref, dens_ref, flip_ref, amp_ref):
    s = pl.program_id(0)
    blocks = pl.num_programs(0)
    row, col = num_ref[0], num_ref[1]
    virtuals = vrow_ref.shape[1]

    @pl.when(s == 0)
    def _():
        gamma_ref[...] = jnp.zeros_like(gamma_ref)
        dens_ref[...] = jnp.zeros_like(dens_ref)
        flip_ref[...] = gr_ref[0].T

    touch = num_ref[2 + s]
    first = num_ref[2 + blocks + s]

    @pl.when(touch > 0)
    def _():
        weight = touch.astype(jnp.float32)
        for i in range(orbitals):
            own = pl.ds(i * virtuals, virtuals)
            k_rows = jnp.dot(flip_ref[own, :], gs_ref[0], preferred_element_type=jnp.float32)
            parts = []
            for j in range(orbitals):
                k_ij = k_rows[:, j * virtuals:(j + 1) * virtuals]
                pair = occ_ref[row * orbitals + i] + occ_ref[s * orbitals + j]
                denominator = (pair - vcol_ref[...]) - vrow_ref[...]
                parts.append(((2.0 * k_ij - k_ij.T) / denominator).astype(jnp.bfloat16))
            amp = jnp.concatenate(parts, axis=1)
            amp_ref[i] = amp
            gamma_ref[:, own] += weight * lax.dot_general(
                gc_ref[0], amp, (((1,), (1,)), ((), ())), preferred_element_type=jnp.float32)

        @pl.when(first > 0)
        def _():
            strip = virtuals // cols
            count = first.astype(jnp.float32)
            for i in range(orbitals):
                mine = amp_ref[i, pl.ds(pl.multiple_of(col * strip, strip), strip), :]
                dens_ref[...] += count * lax.dot_general(
                    mine, amp_ref[i], (((1,), (1,)), ((), ())), preferred_element_type=jnp.float32)


def density_kernel(scale, part_ref, out_ref, arrived, send_sem, take_sem, pass_sem, row_sem, fan_sem, col_sem):
    rows, cols = lax.axis_size("orow"), lax.axis_size("ocol")
    row, col = lax.axis_index("orow"), lax.axis_index("ocol")
    barrier = pltpu.get_barrier_semaphore()

    def peer(step):
        return lax.rem(row + step, rows)

    def other(step):
        return lax.rem(col + step, cols)

    @pl.loop(1, rows)
    def _(step):
        pl.semaphore_signal(barrier, inc=1, device_id={"orow": peer(step)}, device_id_type=MESH)

    @pl.loop(1, cols)
    def _(step):
        pl.semaphore_signal(barrier, inc=1, device_id={"ocol": other(step)}, device_id_type=MESH)

    pl.semaphore_wait(barrier, rows + cols - 2)

    def scatter(step):
        return pltpu.make_async_remote_copy(
            src_ref=part_ref.at[peer(step)], dst_ref=arrived.at[step - 1], send_sem=send_sem.at[step - 1],
            recv_sem=take_sem.at[step - 1], device_id={"orow": peer(step)}, device_id_type=MESH)

    def spread(step):
        spot = out_ref.at[col, row]
        return pltpu.make_async_remote_copy(
            src_ref=spot, dst_ref=spot, send_sem=pass_sem.at[step - 1],
            recv_sem=row_sem.at[step - 1], device_id={"orow": peer(step)}, device_id_type=MESH)

    def fan(step):
        spot = out_ref.at[col]
        return pltpu.make_async_remote_copy(
            src_ref=spot, dst_ref=spot, send_sem=fan_sem.at[step - 1],
            recv_sem=col_sem.at[step - 1], device_id={"ocol": other(step)}, device_id_type=MESH)

    @pl.loop(1, rows)
    def _(step):
        scatter(step).start()

    total = part_ref[row]
    for step in range(1, rows):
        scatter(step).wait()
        total = total + arrived[step - 1]
    out_ref[col, row] = total * scale

    @pl.loop(1, rows)
    def _(step):
        spread(step).start()

    @pl.loop(1, rows)
    def _(step):
        spread(step).wait()

    @pl.loop(1, cols)
    def _(step):
        fan(step).start()

    @pl.loop(1, cols)
    def _(step):
        fan(step).wait()


def sum_density(part, tasks):
    rows, cols = lax.axis_size("orow"), lax.axis_size("ocol")
    strip, virtuals = part.shape
    share = strip // rows
    full = pl.pallas_call(
        functools.partial(density_kernel, 1.0 / tasks),
        out_shape=jax.ShapeDtypeStruct((cols, rows, share, virtuals), jnp.float32),
        in_specs=[pl.BlockSpec(memory_space=pltpu.VMEM)],
        out_specs=pl.BlockSpec(memory_space=pltpu.VMEM),
        scratch_shapes=[
            pltpu.VMEM((rows - 1, share, virtuals), jnp.float32),
            pltpu.SemaphoreType.DMA((rows - 1,)),
            pltpu.SemaphoreType.DMA((rows - 1,)),
            pltpu.SemaphoreType.DMA((rows - 1,)),
            pltpu.SemaphoreType.DMA((rows - 1,)),
            pltpu.SemaphoreType.DMA((cols - 1,)),
            pltpu.SemaphoreType.DMA((cols - 1,)),
        ],
        compiler_params=pltpu.CompilerParams(collective_id=1, has_side_effects=True),
    )(part.reshape(rows, share, virtuals))
    return full.reshape(virtuals, virtuals)


def gather_kernel(nz, nx, ny, cut, shard_ref, all_ref, own_sem, send_sem, line_sem, pair_sem):
    aux_local = shard_ref.shape[0]
    row, col = lax.axis_index("orow"), lax.axis_index("ocol")
    z, x, y, k = row // nx, lax.rem(row, nx), col // 2, lax.rem(col, 2)
    spans = (pl.ds(0, cut), pl.ds(cut, aux_local - cut))

    def turn(at, by, extent):
        return lax.rem(at + by, extent)

    def place(dz=0, dx=0, dy=0):
        return turn(z, dz, nz) * nx + turn(x, dx, nx), turn(y, dy, ny)

    def device(dz=0, dx=0, dy=0, dk=0):
        r, c = place(dz, dx, dy)
        return {"orow": r, "ocol": c * 2 + lax.rem(k + dk, 2)}

    near = sorted(range(1, nz), key=lambda d: min(d, nz - d))
    lines = {
        "z": [dict(dz=d) for d in near],
        "x": [dict(dx=d) for d in range(1, nx)],
        "y": [dict(dy=d) for d in range(1, ny)],
    }
    peers = lines["z"] + lines["x"] + lines["y"] + [dict(dk=1)]
    barrier = pltpu.get_barrier_semaphore()
    for peer in peers:
        pl.semaphore_signal(barrier, inc=1, device_id=device(**peer), device_id_type=MESH)
    pl.semaphore_wait(barrier, len(peers))

    sent = []

    def push(piece, at, source, sem, peer):
        r, c = place(**at)
        copy = pltpu.make_async_remote_copy(
            src_ref=source, dst_ref=all_ref.at[r, c * 2 + k, spans[piece]], send_sem=send_sem.at[len(sent)],
            recv_sem=sem, device_id=device(**peer), device_id_type=MESH)
        copy.start()
        sent.append(copy)

    def pass_on(piece, at, order):
        r, c = place(**at)
        own = not at
        source = shard_ref.at[spans[piece]] if own else all_ref.at[r, c * 2 + k, spans[piece]]
        for axis in order:
            for peer in lines[axis]:
                push(piece, at, source, line_sem.at[piece, r, c], peer)
        push(piece, at, source, pair_sem.at[piece, r, c], dict(dk=1))

    def take(piece, at, sem, core):
        r, c = place(**at)
        spot = all_ref.at[r, c * 2 + core, spans[piece]]
        pltpu.make_async_remote_copy(
            src_ref=spot, dst_ref=spot, send_sem=send_sem.at[0], recv_sem=sem.at[piece, r, c],
            device_id=device(dk=1), device_id_type=MESH).wait_recv()

    def relay(piece, at, order):
        take(piece, at, line_sem, k)
        pass_on(piece, at, order)

    keep = pltpu.make_async_copy(shard_ref, all_ref.at[row, col], own_sem)
    keep.start()
    pass_on(1, {}, "yzx")
    pass_on(0, {}, "zxy")
    for side in lines["y"]:
        relay(1, side, "zx")
    for up in lines["z"]:
        relay(0, up, "xy")
    for up in [{}] + lines["z"]:
        for across in lines["x"]:
            relay(0, up | across, "y")
        if up:
            for side in [{}] + lines["y"]:
                relay(1, up | side, "x")
    for up in [{}] + lines["z"]:
        for across in [{}] + lines["x"]:
            for side in lines["y"]:
                relay(0, up | across | side, "")
        for side in [{}] + lines["y"]:
            for across in lines["x"]:
                relay(1, up | across | side, "")
    for dz in range(nz):
        for dx in range(nx):
            for dy in range(ny):
                for piece in (0, 1):
                    take(piece, dict(dz=dz, dx=dx, dy=dy), pair_sem, 1 - k)
    keep.wait()
    for copy in sent:
        copy.wait_send()


def gather_all(shard):
    rows, cols = lax.axis_size("orow"), lax.axis_size("ocol")
    ny = cols // 2
    nx = ny if rows % ny == 0 else 1
    nz = rows // nx
    aux_local, span = shard.shape
    cut = aux_local * 7 // 11 // 16 * 16
    pushes = 2 * nz * nx * ny + (nz - 1) + nz * (nx - 1) + nz * nx * (ny - 1) + (ny - 1) + ny * (nz - 1) + nz * ny * (nx - 1)
    return pl.pallas_call(
        functools.partial(gather_kernel, nz, nx, ny, cut),
        out_shape=jax.ShapeDtypeStruct((rows, cols, aux_local, span), shard.dtype),
        in_specs=[pl.BlockSpec(memory_space=pltpu.VMEM)],
        out_specs=pl.BlockSpec(memory_space=pl.ANY),
        scratch_shapes=[
            pltpu.SemaphoreType.DMA,
            pltpu.SemaphoreType.DMA((pushes,)),
            pltpu.SemaphoreType.DMA((2, rows, ny)),
            pltpu.SemaphoreType.DMA((2, rows, ny)),
        ],
        compiler_params=pltpu.CompilerParams(collective_id=2, has_side_effects=True),
    )(shard)


def fused_kernel(nz, nx, tasks, shard_ref, count_ref, occ_ref, ti_ref, tj_ref, vir_ref, out_ref, dens_ref,
                 mine, rows_ref, cols_ref, flips, vsum, amp, total, stage, xmsg, ymsg, keep, fold, part, gath, strip, plane,
                 row_sem, col_sem, x_sem, y_sem, keep_sem, fold_sem, part_sem, plane_sem, line_sem, dens_sem,
                 first_send, relay_send, pass_send, gamma_send, fold_send, part_send, plane_send, col_send, dens_send, home_sem):
    _, virtuals, aux = flips.shape
    row, col = lax.axis_index("orow"), lax.axis_index("ocol")
    z, x, y, k = row // nx, lax.rem(row, nx), col // 2, lax.rem(col, 2)
    nx_, ny_, nk_ = 1 - x, 1 - y, 1 - k
    parity = lax.rem(z, 2)
    twin, mirror = z + 1 - 2 * parity, nz - 1 - z
    owner = parity == k
    other = jnp.logical_not(owner)
    both = jnp.logical_and
    dif = lax.rem(parity + k, 2)
    block = (z - parity + k) * nx + x
    cores = (k, nk_)

    def device(dz, dx, dy, dk):
        return {"orow": dz * nx + dx, "ocol": dy * 2 + dk}

    def remote(src, dst, send, take, where):
        return pltpu.make_async_remote_copy(
            src_ref=src, dst_ref=dst, send_sem=send, recv_sem=take, device_id=where, device_id_type=MESH)

    sibling = device(z, x, y, nk_)

    def arrive(ref, sem):
        remote(ref, ref, first_send.at[0], sem, sibling).wait_recv()

    barrier = pltpu.get_barrier_semaphore()
    peers = [sibling, device(nz - 1 - twin, x, y, k)]
    for c in range(2):
        peers += [device(z, x, ny_, c), device(z, nx_, y, c), device(twin, x, y, c), device(mirror, x, y, c)]
    for peer in peers:
        pl.semaphore_signal(barrier, inc=1, device_id=peer, device_id_type=MESH)

    count = count_ref[row]
    for r in range(2):
        o = lax.rem(y + r, 2)
        active = jnp.where(count > o, 1.0, 0.0).astype(jnp.float32)
        mine[r] = (shard_ref[o].astype(jnp.float32) * active).astype(jnp.bfloat16)
    cols_ref[0, 0] = mine[0]

    @pl.when(owner)
    def _():
        for r in range(2):
            rows_ref[r, 0] = mine[r]

    pl.semaphore_wait(barrier, len(peers))

    def give_row(source, r, q, where, slot):
        return remote(mine.at[source], rows_ref.at[r, q], first_send.at[slot], row_sem.at[r, q], where)

    def give_col(zr, q, where, slot):
        return remote(mine.at[0], cols_ref.at[zr, q], first_send.at[slot], col_sem.at[zr, q], where)

    opening = [
        give_col(2, 0, device(mirror, x, y, k), 3),
        give_row(1, 0, 2 + dif, device(z, x, ny_, parity), 0),
        give_col(1, 0, device(z, nx_, y, k), 2),
        give_row(0, 1, 2 + dif, device(z, x, ny_, parity), 5),
        give_row(1, 1, dif, device(twin, x, y, parity), 6),
        give_row(0, 0, dif, device(twin, x, y, parity), 1),
        give_col(0, 1, sibling, 4),
    ]
    home = [give_row(0, 0, 1, sibling, 7), give_row(1, 1, 1, sibling, 8)]
    for copy in opening:
        copy.start()

    @pl.when(other)
    def _():
        for copy in home:
            copy.start()

    def wait_row(r, q):
        arrive(rows_ref.at[r, q], row_sem.at[r, q])

    def wait_col(zr, q):
        arrive(cols_ref.at[zr, q], col_sem.at[zr, q])

    def relays(c):
        source = rows_ref.at[0, 2 + c]
        return [
            remote(source, cols_ref.at[2, 2], relay_send.at[c, 1], col_sem.at[2, 2], device(mirror, x, y, cores[c])),
            remote(source, cols_ref.at[1, 2], relay_send.at[c, 0], col_sem.at[1, 2], device(z, nx_, y, cores[c])),
            remote(source, cols_ref.at[0, 3 - c], relay_send.at[c, 3], col_sem.at[0, 3 - c], sibling),
        ]

    def at_home(c):
        return pltpu.make_async_copy(rows_ref.at[0, 2 + c], cols_ref.at[0, 2 + c], home_sem.at[c])

    def across(r, c):
        return remote(rows_ref.at[r, c], rows_ref.at[1 - r, 2 + c], relay_send.at[c, r], row_sem.at[1 - r, 2 + c],
                      device(z, x, ny_, k))

    @pl.when(owner)
    def _():
        for c in range(2):
            wait_row(0, 2 + c)
            for copy in relays(c):
                copy.start()
            at_home(c).start()

    @pl.when(other)
    def _():
        for r in (1, 0):
            for c in range(2):
                wait_row(r, c)
                across(r, c).start()

    places = (z * nx + x, z * nx + nx_, mirror * nx + x, mirror * nx + nx_)

    def tally(t, carry):
        a, b = ti_ref[t], tj_ref[t]
        result = []
        for zr, j in enumerate(places):
            ahead = jnp.where(a == block, 1, 0) * jnp.where(b == j, 1, 0)
            behind = jnp.where(b == block, 1, 0) * jnp.where(a == j, 1, 0)
            result += [carry[2 * zr] + ahead, carry[2 * zr + 1] + behind]
        return tuple(result)

    tallies = lax.fori_loop(0, tasks, tally, (jnp.int32(0),) * (2 * nz))
    ahead = [tallies[2 * zr].astype(jnp.float32) for zr in range(nz)]
    weight = [(tallies[2 * zr] + tallies[2 * zr + 1]).astype(jnp.float32) for zr in range(nz)]
    spread = jnp.broadcast_to(vir_ref[...].reshape(1, virtuals), vsum.shape)
    vsum[...] = spread + spread.T

    def pass_on(zr, a, slot):
        q = 2 * a
        return remote(cols_ref.at[zr, q], cols_ref.at[zr, q + 1], pass_send.at[slot], col_sem.at[zr, q + 1], sibling)

    passed = []

    def launch(copy):
        copy.start()
        passed.append(copy)

    def take(zr, a):
        q = 2 * a
        wait_col(zr, q)
        if zr == 2:
            launch(remote(cols_ref.at[2, q], cols_ref.at[3, q], pass_send.at[len(passed)], col_sem.at[3, q],
                          device(z, nx_, y, k)))
        launch(pass_on(zr, a, len(passed)))

    def amplitudes(r, zr):
        kij = jnp.dot(flips[r], cols_ref[zr].reshape(aux, virtuals), preferred_element_type=jnp.float32)
        pair = occ_ref[block * 2 + lax.rem(y + r, 2)] + occ_ref[places[zr] * 2 + y]
        amp[zr, r] = ((2.0 * kij - kij.T) / (pair - vsum[...])).astype(jnp.bfloat16)

    take(1, 0)
    take(2, 0)
    take(1, 1)
    take(2, 1)

    @pl.when(owner)
    def _():
        wait_row(0, 1)

    @pl.when(other)
    def _():
        for c in range(2):
            wait_row(0, 2 + c)

    flips[0] = rows_ref[0].reshape(aux, virtuals).T
    wait_col(0, 1)

    @pl.when(owner)
    def _():
        for c in range(2):
            at_home(c).wait()

    @pl.when(other)
    def _():
        for c in range(2):
            wait_col(0, 2 + c)

    amplitudes(0, 0)
    for q in (1, 3):
        wait_col(1, q)
    amplitudes(0, 1)
    take(3, 0)
    for q in (1, 3):
        wait_col(2, q)
    amplitudes(0, 2)
    @pl.when(owner)
    def _():
        for q in (1, 2, 3):
            wait_row(1, q)

    @pl.when(other)
    def _():
        for q in (2, 3):
            wait_row(1, q)

    flips[1] = rows_ref[1].reshape(aux, virtuals).T
    for zr in range(2):
        amplitudes(1, zr)
    take(3, 1)
    for q in (1, 3):
        wait_col(3, q)
    amplitudes(0, 3)

    def gamma_sends(r, a, c):
        over_z, over_y = k == c, k == 1 - c
        q = 2 * a + c
        src, send = stage.at[r, q], gamma_send.at[r, q]
        if a == 0:
            sends = [(both(other, over_z), remote(src, xmsg.at[r], send, x_sem.at[r], device(twin, x, y, cores[c])))]
            if c == 1:
                sends.append((owner, remote(total.at[r, q], keep.at[r], send, keep_sem.at[r], sibling)))
            return sends
        return [
            (both(other, over_z), remote(src, fold.at[r], send, fold_sem.at[r], device(twin, x, y, k))),
            (both(other, over_y), remote(src, fold.at[1 - r], send, fold_sem.at[1 - r], device(z, x, ny_, k))),
            (both(owner, over_y), remote(src, ymsg.at[1 - r], send, y_sem.at[1 - r], device(z, x, ny_, cores[c]))),
        ]

    def guarded(condition, action):
        @pl.when(condition)
        def _():
            action()

    def send_off(r, a, c):
        for condition, copy in gamma_sends(r, a, c):
            guarded(condition, copy.start)

    def gamma(r, a, hold=False):
        for c in range(2):
            q = 2 * a + c
            value = weight[0] * lax.dot_general(
                cols_ref[0, q], amp[0, r], (((1,), (1,)), ((), ())), preferred_element_type=jnp.float32)
            for zr in range(1, nz):
                value += weight[zr] * lax.dot_general(
                    cols_ref[zr, q], amp[zr, r], (((1,), (1,)), ((), ())), preferred_element_type=jnp.float32)
            total[r, q] = value
            stage[r, q] = value.astype(jnp.bfloat16)
            if q == 0:
                @pl.when(owner)
                def _():
                    keep[r] = value

            if not hold:
                send_off(r, a, c)

    def folded(own, r, c):
        if own:
            return remote(stage.at[r, 2 + c], ymsg.at[1 - r], fold_send.at[r], y_sem.at[1 - r], device(z, x, ny_, cores[c]))
        return remote(stage.at[r, c], xmsg.at[r], fold_send.at[r], x_sem.at[r], device(twin, x, y, cores[c]))

    def holders(own):
        return [(c, both(owner, k == c) if own else both(other, k == 1 - c)) for c in range(2)]

    def fold_in(own, r):
        for c, condition in holders(own):
            @pl.when(condition)
            def _():
                arrive(fold.at[r], fold_sem.at[r])
                q = (2 if own else 0) + c
                stage[r, q] = (total[r, q] + fold[r].astype(jnp.float32)).astype(jnp.bfloat16)
                folded(own, r, c).start()

    gamma(0, 1)

    for zr in range(2, nz):
        amplitudes(1, zr)

    gamma(1, 1)

    def square(zr):
        return sum(lax.dot_general(amp[zr, r], amp[zr, r], (((1,), (1,)), ((), ())),
                                   preferred_element_type=jnp.float32) for r in range(2))

    dens = ahead[0] * square(0)
    for zr in range(1, nz):
        dens += ahead[zr] * square(zr)
    part[...] = dens.reshape(part.shape)
    me = x * 2 + k
    quad = []
    for dx in range(2):
        for dk in range(2):
            if dx or dk:
                tx, tk = lax.rem(x + dx, 2), lax.rem(k + dk, 2)
                quad.append((dx * 2 + dk, tx * 2 + tk, device(z, tx, y, tk)))
    line = [(slot, dz, device(dz, x, y, k)) for slot, dz in ((1, twin), (2, mirror), (3, nz - 1 - twin))]
    pair = remote(plane.at[5], plane.at[4], plane_send.at[3], plane_sem.at[4], device(z, x, ny_, k))

    def scatter(slot, there, where):
        return remote(part.at[there], gath.at[slot], part_send.at[slot - 1], part_sem.at[slot], where)

    def swap(slot, dz, where):
        return remote(strip.at[dz], plane.at[slot], plane_send.at[slot - 1], plane_sem.at[slot], where)

    def collect(slot, dz, where):
        return remote(dens_ref.at[me, z], dens_ref.at[me, z], col_send.at[slot - 1], line_sem.at[z], where)

    def spread_out(slot, there, where):
        return remote(dens_ref.at[me], dens_ref.at[me], dens_send.at[slot - 1], dens_sem.at[me], where)

    for item in quad:
        scatter(*item).start()
    gath[0] = part[me]
    gamma(0, 0, True)
    for slot, there, where in quad:
        arrive(gath.at[slot], part_sem.at[slot])
    strip[...] = (gath[0] + gath[1]) + (gath[2] + gath[3])
    for item in line:
        swap(*item).start()
    plane[0] = strip[z]
    for c in range(2):
        send_off(0, 0, c)
    fold_in(True, 0)
    gamma(1, 0)
    for slot, dz, where in line:
        arrive(plane.at[slot], plane_sem.at[slot])
    plane[5] = (plane[0] + plane[1]) + (plane[2] + plane[3])
    pair.start()
    arrive(plane.at[4], plane_sem.at[4])
    dens_ref[me, z] = (plane[4] + plane[5]) * (1.0 / tasks)
    for item in line:
        collect(*item).start()
    fold_in(False, 1)
    fold_in(True, 1)
    fold_in(False, 0)
    for slot, dz, where in line:
        arrive(dens_ref.at[me, dz], line_sem.at[dz])
    for item in quad:
        spread_out(*item).start()

    for r in range(2):
        guarded(other, lambda: arrive(keep.at[r], keep_sem.at[r]))
        arrive(xmsg.at[r], x_sem.at[r])
        arrive(ymsg.at[r], y_sem.at[r])
    for o in range(2):
        r = lax.rem(y + o, 2)
        out_ref[:, o, :] = (keep[r] + xmsg[r].astype(jnp.float32)) + ymsg[r].astype(jnp.float32)

    for slot, there, where in quad:
        arrive(dens_ref.at[there], dens_sem.at[there])
    for copy in opening + passed:
        copy.wait_send()

    @pl.when(other)
    def _():
        for copy in home:
            copy.wait_send()
        for r in range(2):
            for c in range(2):
                across(r, c).wait_send()

    @pl.when(owner)
    def _():
        for c in range(2):
            for copy in relays(c):
                copy.wait_send()

    for r in range(2):
        for a in range(2):
            for c in range(2):
                for condition, copy in gamma_sends(r, a, c):
                    guarded(condition, copy.wait_send)
    for own in (True, False):
        for c, condition in holders(own):
            for r in range(2):
                guarded(condition, folded(own, r, c).wait_send)
    for item in quad:
        scatter(*item).wait_send()
        spread_out(*item).wait_send()
    for item in line:
        swap(*item).wait_send()
        collect(*item).wait_send()
    pair.wait_send()


def fused(integrals, occ_count, occ_energy, vir_energy, task_iblock, task_jblock, nz, nx):
    aux_local, orbitals, virtuals = integrals.shape
    aux = aux_local * lax.axis_size("ocol")
    tasks = task_jblock.shape[0]
    share = virtuals // (4 * nz)
    half, full = jnp.bfloat16, jnp.float32
    dma = pltpu.SemaphoreType.DMA
    vmem, smem = pl.BlockSpec(memory_space=pltpu.VMEM), pl.BlockSpec(memory_space=pltpu.SMEM)
    out, dens = pl.pallas_call(
        functools.partial(fused_kernel, nz, nx, tasks),
        out_shape=[
            jax.ShapeDtypeStruct((aux_local, orbitals, virtuals), full),
            jax.ShapeDtypeStruct((4, nz, share, virtuals), full),
        ],
        in_specs=[vmem, smem, smem, smem, smem, vmem],
        out_specs=[vmem, vmem],
        scratch_shapes=[
            pltpu.VMEM((2, aux_local, virtuals), half),
            pltpu.VMEM((2, 4, aux_local, virtuals), half),
            pltpu.VMEM((nz, 4, aux_local, virtuals), half),
            pltpu.VMEM((2, virtuals, aux), half),
            pltpu.VMEM((virtuals, virtuals), full),
            pltpu.VMEM((nz, 2, virtuals, virtuals), half),
            pltpu.VMEM((2, 4, aux_local, virtuals), full),
            pltpu.VMEM((2, 4, aux_local, virtuals), half),
            pltpu.VMEM((2, aux_local, virtuals), half),
            pltpu.VMEM((2, aux_local, virtuals), half),
            pltpu.VMEM((2, aux_local, virtuals), full),
            pltpu.VMEM((2, aux_local, virtuals), half),
            pltpu.VMEM((4, nz, share, virtuals), full),
            pltpu.VMEM((4, nz, share, virtuals), full),
            pltpu.VMEM((nz, share, virtuals), full),
            pltpu.VMEM((nz + 2, share, virtuals), full),
            dma((2, 4)), dma((nz, 4)), dma((2,)), dma((2,)), dma((2,)), dma((2,)), dma((4,)), dma((2 * nz,)), dma((nz,)), dma((4,)),
            dma((9,)), dma((2, 4)), dma((8,)), dma((2, 4)), dma((2,)), dma((3,)), dma((2 * nz - 1,)), dma((nz - 1,)), dma((3,)), dma((2,)),
        ],
        compiler_params=pltpu.CompilerParams(
            collective_id=3, has_side_effects=True, vmem_limit_bytes=56 * 1024 * 1024),
    )(jnp.transpose(integrals, (1, 0, 2)), occ_count, occ_energy, task_iblock[:, 0], task_jblock, vir_energy)
    return out, dens.reshape(virtuals, virtuals)


def local(integrals, occ_count, occ_energy, vir_energy, task_iblock, task_jblock):
    aux_local, orbitals, virtuals = integrals.shape
    span = orbitals * virtuals
    blocks = lax.axis_size("orow")
    cols = lax.axis_size("ocol")
    if blocks == 8 and cols == 4 and orbitals == 2:
        return fused(integrals, occ_count, occ_energy, vir_energy, task_iblock, task_jblock, blocks // 2, 2)
    row = lax.axis_index("orow")
    col = lax.axis_index("ocol")
    aux = aux_local * cols
    active = jnp.arange(orbitals) < occ_count[row]
    masked = integrals * active.astype(jnp.bfloat16)[None, :, None]
    shard = masked.reshape(aux_local, span)
    gathered = gather_all(shard).reshape(blocks, aux, span)
    i_list, j_list = task_iblock[:, 0], task_jblock
    ids = jnp.arange(blocks)
    i_hot = i_list[None, :] == ids[:, None]
    j_hot = j_list[None, :] == ids[:, None]
    first = jnp.sum((i_list == row)[None, :] & j_hot, axis=1).astype(jnp.int32)
    second = jnp.sum((j_list == row)[None, :] & i_hot, axis=1).astype(jnp.int32)
    numbers = jnp.concatenate([jnp.stack([row, col]).astype(jnp.int32), first + second, first])
    gamma, dens = pl.pallas_call(
        functools.partial(pair_kernel, orbitals, cols),
        grid_spec=pltpu.PrefetchScalarGridSpec(
            num_scalar_prefetch=2,
            grid=(blocks,),
            in_specs=[
                pl.BlockSpec((1, aux, span), lambda s, num, occ: (num[0], 0, 0)),
                pl.BlockSpec((1, aux, span), lambda s, num, occ: (s, 0, 0)),
                pl.BlockSpec((1, aux_local, span), lambda s, num, occ: (s, num[1], 0)),
                pl.BlockSpec((1, virtuals), lambda s, num, occ: (0, 0)),
                pl.BlockSpec((virtuals, 1), lambda s, num, occ: (0, 0)),
            ],
            out_specs=[
                pl.BlockSpec((aux_local, span), lambda s, num, occ: (0, 0)),
                pl.BlockSpec((virtuals // cols, virtuals), lambda s, num, occ: (0, 0)),
            ],
            scratch_shapes=[pltpu.VMEM((span, aux), jnp.bfloat16), pltpu.VMEM((orbitals, virtuals, span), jnp.bfloat16)],
        ),
        out_shape=[
            jax.ShapeDtypeStruct((aux_local, span), jnp.float32),
            jax.ShapeDtypeStruct((virtuals // cols, virtuals), jnp.float32),
        ],
        compiler_params=pltpu.CompilerParams(vmem_limit_bytes=56 * 1024 * 1024),
    )(numbers, occ_energy, gathered, gathered, gathered, vir_energy[None, :], vir_energy[:, None])
    density = sum_density(dens, i_list.shape[0])
    return gamma.reshape(aux_local, orbitals, virtuals), density


def solution(mesh):
    return jax.shard_map(
        local,
        mesh=mesh,
        in_specs=(P("ocol", "orow", None), P(), P(), P(), P(), P()),
        out_specs=(P("ocol", "orow", None), P()),
        check_vma=False,
    )
```

```python
import functools

import jax
import jax.numpy as jnp
from jax import lax
from jax.experimental import pallas as pl
from jax.experimental.pallas import tpu as pltpu
from jax.sharding import PartitionSpec as P

MESH = pl.DeviceIdType.MESH


def pair_kernel(orbitals, cols, num_ref, occ_ref, gr_ref, gs_ref, gc_ref, vrow_ref, vcol_ref, gamma_ref, dens_ref, flip_ref, amp_ref):
    s = pl.program_id(0)
    blocks = pl.num_programs(0)
    row, col = num_ref[0], num_ref[1]
    virtuals = vrow_ref.shape[1]

    @pl.when(s == 0)
    def _():
        gamma_ref[...] = jnp.zeros_like(gamma_ref)
        dens_ref[...] = jnp.zeros_like(dens_ref)
        flip_ref[...] = gr_ref[0].T

    touch = num_ref[2 + s]
    first = num_ref[2 + blocks + s]

    @pl.when(touch > 0)
    def _():
        weight = touch.astype(jnp.float32)
        for i in range(orbitals):
            own = pl.ds(i * virtuals, virtuals)
            k_rows = jnp.dot(flip_ref[own, :], gs_ref[0], preferred_element_type=jnp.float32)
            parts = []
            for j in range(orbitals):
                k_ij = k_rows[:, j * virtuals:(j + 1) * virtuals]
                pair = occ_ref[row * orbitals + i] + occ_ref[s * orbitals + j]
                denominator = (pair - vcol_ref[...]) - vrow_ref[...]
                parts.append(((2.0 * k_ij - k_ij.T) / denominator).astype(jnp.bfloat16))
            amp = jnp.concatenate(parts, axis=1)
            amp_ref[i] = amp
            gamma_ref[:, own] += weight * lax.dot_general(
                gc_ref[0], amp, (((1,), (1,)), ((), ())), preferred_element_type=jnp.float32)

        @pl.when(first > 0)
        def _():
            strip = virtuals // cols
            count = first.astype(jnp.float32)
            for i in range(orbitals):
                mine = amp_ref[i, pl.ds(pl.multiple_of(col * strip, strip), strip), :]
                dens_ref[...] += count * lax.dot_general(
                    mine, amp_ref[i], (((1,), (1,)), ((), ())), preferred_element_type=jnp.float32)


def density_kernel(scale, part_ref, out_ref, arrived, send_sem, take_sem, pass_sem, row_sem, fan_sem, col_sem):
    rows, cols = lax.axis_size("orow"), lax.axis_size("ocol")
    row, col = lax.axis_index("orow"), lax.axis_index("ocol")
    barrier = pltpu.get_barrier_semaphore()

    def peer(step):
        return lax.rem(row + step, rows)

    def other(step):
        return lax.rem(col + step, cols)

    @pl.loop(1, rows)
    def _(step):
        pl.semaphore_signal(barrier, inc=1, device_id={"orow": peer(step)}, device_id_type=MESH)

    @pl.loop(1, cols)
    def _(step):
        pl.semaphore_signal(barrier, inc=1, device_id={"ocol": other(step)}, device_id_type=MESH)

    pl.semaphore_wait(barrier, rows + cols - 2)

    def scatter(step):
        return pltpu.make_async_remote_copy(
            src_ref=part_ref.at[peer(step)], dst_ref=arrived.at[step - 1], send_sem=send_sem.at[step - 1],
            recv_sem=take_sem.at[step - 1], device_id={"orow": peer(step)}, device_id_type=MESH)

    def spread(step):
        spot = out_ref.at[col, row]
        return pltpu.make_async_remote_copy(
            src_ref=spot, dst_ref=spot, send_sem=pass_sem.at[step - 1],
            recv_sem=row_sem.at[step - 1], device_id={"orow": peer(step)}, device_id_type=MESH)

    def fan(step):
        spot = out_ref.at[col]
        return pltpu.make_async_remote_copy(
            src_ref=spot, dst_ref=spot, send_sem=fan_sem.at[step - 1],
            recv_sem=col_sem.at[step - 1], device_id={"ocol": other(step)}, device_id_type=MESH)

    @pl.loop(1, rows)
    def _(step):
        scatter(step).start()

    total = part_ref[row]
    for step in range(1, rows):
        scatter(step).wait()
        total = total + arrived[step - 1]
    out_ref[col, row] = total * scale

    @pl.loop(1, rows)
    def _(step):
        spread(step).start()

    @pl.loop(1, rows)
    def _(step):
        spread(step).wait()

    @pl.loop(1, cols)
    def _(step):
        fan(step).start()

    @pl.loop(1, cols)
    def _(step):
        fan(step).wait()


def sum_density(part, tasks):
    rows, cols = lax.axis_size("orow"), lax.axis_size("ocol")
    strip, virtuals = part.shape
    share = strip // rows
    full = pl.pallas_call(
        functools.partial(density_kernel, 1.0 / tasks),
        out_shape=jax.ShapeDtypeStruct((cols, rows, share, virtuals), jnp.float32),
        in_specs=[pl.BlockSpec(memory_space=pltpu.VMEM)],
        out_specs=pl.BlockSpec(memory_space=pltpu.VMEM),
        scratch_shapes=[
            pltpu.VMEM((rows - 1, share, virtuals), jnp.float32),
            pltpu.SemaphoreType.DMA((rows - 1,)),
            pltpu.SemaphoreType.DMA((rows - 1,)),
            pltpu.SemaphoreType.DMA((rows - 1,)),
            pltpu.SemaphoreType.DMA((rows - 1,)),
            pltpu.SemaphoreType.DMA((cols - 1,)),
            pltpu.SemaphoreType.DMA((cols - 1,)),
        ],
        compiler_params=pltpu.CompilerParams(collective_id=1, has_side_effects=True),
    )(part.reshape(rows, share, virtuals))
    return full.reshape(virtuals, virtuals)


def gather_kernel(nz, nx, ny, cut, shard_ref, all_ref, own_sem, send_sem, line_sem, pair_sem):
    aux_local = shard_ref.shape[0]
    row, col = lax.axis_index("orow"), lax.axis_index("ocol")
    z, x, y, k = row // nx, lax.rem(row, nx), col // 2, lax.rem(col, 2)
    spans = (pl.ds(0, cut), pl.ds(cut, aux_local - cut))

    def turn(at, by, extent):
        return lax.rem(at + by, extent)

    def place(dz=0, dx=0, dy=0):
        return turn(z, dz, nz) * nx + turn(x, dx, nx), turn(y, dy, ny)

    def device(dz=0, dx=0, dy=0, dk=0):
        r, c = place(dz, dx, dy)
        return {"orow": r, "ocol": c * 2 + lax.rem(k + dk, 2)}

    near = sorted(range(1, nz), key=lambda d: min(d, nz - d))
    lines = {
        "z": [dict(dz=d) for d in near],
        "x": [dict(dx=d) for d in range(1, nx)],
        "y": [dict(dy=d) for d in range(1, ny)],
    }
    peers = lines["z"] + lines["x"] + lines["y"] + [dict(dk=1)]
    barrier = pltpu.get_barrier_semaphore()
    for peer in peers:
        pl.semaphore_signal(barrier, inc=1, device_id=device(**peer), device_id_type=MESH)
    pl.semaphore_wait(barrier, len(peers))

    sent = []

    def push(piece, at, source, sem, peer):
        r, c = place(**at)
        copy = pltpu.make_async_remote_copy(
            src_ref=source, dst_ref=all_ref.at[r, c * 2 + k, spans[piece]], send_sem=send_sem.at[len(sent)],
            recv_sem=sem, device_id=device(**peer), device_id_type=MESH)
        copy.start()
        sent.append(copy)

    def pass_on(piece, at, order):
        r, c = place(**at)
        own = not at
        source = shard_ref.at[spans[piece]] if own else all_ref.at[r, c * 2 + k, spans[piece]]
        for axis in order:
            for peer in lines[axis]:
                push(piece, at, source, line_sem.at[piece, r, c], peer)
        push(piece, at, source, pair_sem.at[piece, r, c], dict(dk=1))

    def take(piece, at, sem, core):
        r, c = place(**at)
        spot = all_ref.at[r, c * 2 + core, spans[piece]]
        pltpu.make_async_remote_copy(
            src_ref=spot, dst_ref=spot, send_sem=send_sem.at[0], recv_sem=sem.at[piece, r, c],
            device_id=device(dk=1), device_id_type=MESH).wait_recv()

    def relay(piece, at, order):
        take(piece, at, line_sem, k)
        pass_on(piece, at, order)

    keep = pltpu.make_async_copy(shard_ref, all_ref.at[row, col], own_sem)
    keep.start()
    pass_on(1, {}, "yzx")
    pass_on(0, {}, "zxy")
    for side in lines["y"]:
        relay(1, side, "zx")
    for up in lines["z"]:
        relay(0, up, "xy")
    for up in [{}] + lines["z"]:
        for across in lines["x"]:
            relay(0, up | across, "y")
        if up:
            for side in [{}] + lines["y"]:
                relay(1, up | side, "x")
    for up in [{}] + lines["z"]:
        for across in [{}] + lines["x"]:
            for side in lines["y"]:
                relay(0, up | across | side, "")
        for side in [{}] + lines["y"]:
            for across in lines["x"]:
                relay(1, up | across | side, "")
    for dz in range(nz):
        for dx in range(nx):
            for dy in range(ny):
                for piece in (0, 1):
                    take(piece, dict(dz=dz, dx=dx, dy=dy), pair_sem, 1 - k)
    keep.wait()
    for copy in sent:
        copy.wait_send()


def gather_all(shard):
    rows, cols = lax.axis_size("orow"), lax.axis_size("ocol")
    ny = cols // 2
    nx = ny if rows % ny == 0 else 1
    nz = rows // nx
    aux_local, span = shard.shape
    cut = aux_local * 7 // 11 // 16 * 16
    pushes = 2 * nz * nx * ny + (nz - 1) + nz * (nx - 1) + nz * nx * (ny - 1) + (ny - 1) + ny * (nz - 1) + nz * ny * (nx - 1)
    return pl.pallas_call(
        functools.partial(gather_kernel, nz, nx, ny, cut),
        out_shape=jax.ShapeDtypeStruct((rows, cols, aux_local, span), shard.dtype),
        in_specs=[pl.BlockSpec(memory_space=pltpu.VMEM)],
        out_specs=pl.BlockSpec(memory_space=pl.ANY),
        scratch_shapes=[
            pltpu.SemaphoreType.DMA,
            pltpu.SemaphoreType.DMA((pushes,)),
            pltpu.SemaphoreType.DMA((2, rows, ny)),
            pltpu.SemaphoreType.DMA((2, rows, ny)),
        ],
        compiler_params=pltpu.CompilerParams(collective_id=2, has_side_effects=True),
    )(shard)


def fused_kernel(nz, nx, tasks, shard_ref, count_ref, occ_ref, ti_ref, tj_ref, vir_ref, out_ref, dens_ref,
                 mine, rows_ref, cols_ref, flips, vsum, amp, total, stage, xmsg, ymsg, keep, fold, part, gath, strip, plane,
                 row_sem, col_sem, x_sem, y_sem, keep_sem, fold_sem, part_sem, plane_sem, line_sem, dens_sem,
                 first_send, relay_send, pass_send, gamma_send, fold_send, part_send, plane_send, col_send, dens_send, home_sem):
    _, virtuals, aux = flips.shape
    row, col = lax.axis_index("orow"), lax.axis_index("ocol")
    z, x, y, k = row // nx, lax.rem(row, nx), col // 2, lax.rem(col, 2)
    nx_, ny_, nk_ = 1 - x, 1 - y, 1 - k
    parity = lax.rem(z, 2)
    twin, mirror = z + 1 - 2 * parity, nz - 1 - z
    owner = parity == k
    other = jnp.logical_not(owner)
    both = jnp.logical_and
    dif = lax.rem(parity + k, 2)
    block = (z - parity + k) * nx + x
    cores = (k, nk_)

    def device(dz, dx, dy, dk):
        return {"orow": dz * nx + dx, "ocol": dy * 2 + dk}

    def remote(src, dst, send, take, where):
        return pltpu.make_async_remote_copy(
            src_ref=src, dst_ref=dst, send_sem=send, recv_sem=take, device_id=where, device_id_type=MESH)

    sibling = device(z, x, y, nk_)

    def arrive(ref, sem):
        remote(ref, ref, first_send.at[0], sem, sibling).wait_recv()

    barrier = pltpu.get_barrier_semaphore()
    peers = [sibling, device(nz - 1 - twin, x, y, k)]
    for c in range(2):
        peers += [device(z, x, ny_, c), device(z, nx_, y, c), device(twin, x, y, c), device(mirror, x, y, c)]
    for peer in peers:
        pl.semaphore_signal(barrier, inc=1, device_id=peer, device_id_type=MESH)

    count = count_ref[row]
    for r in range(2):
        o = lax.rem(y + r, 2)
        active = jnp.where(count > o, 1.0, 0.0).astype(jnp.float32)
        mine[r] = (shard_ref[o].astype(jnp.float32) * active).astype(jnp.bfloat16)
    cols_ref[0, 0] = mine[0]

    @pl.when(owner)
    def _():
        for r in range(2):
            rows_ref[r, 0] = mine[r]

    pl.semaphore_wait(barrier, len(peers))

    def give_row(source, r, q, where, slot):
        return remote(mine.at[source], rows_ref.at[r, q], first_send.at[slot], row_sem.at[r, q], where)

    def give_col(zr, q, where, slot):
        return remote(mine.at[0], cols_ref.at[zr, q], first_send.at[slot], col_sem.at[zr, q], where)

    opening = [
        give_col(2, 0, device(mirror, x, y, k), 3),
        give_row(1, 0, 2 + dif, device(z, x, ny_, parity), 0),
        give_col(1, 0, device(z, nx_, y, k), 2),
        give_row(0, 1, 2 + dif, device(z, x, ny_, parity), 5),
        give_row(1, 1, dif, device(twin, x, y, parity), 6),
        give_row(0, 0, dif, device(twin, x, y, parity), 1),
        give_col(0, 1, sibling, 4),
    ]
    home = [give_row(0, 0, 1, sibling, 7), give_row(1, 1, 1, sibling, 8)]
    for copy in opening:
        copy.start()

    @pl.when(other)
    def _():
        for copy in home:
            copy.start()

    def wait_row(r, q):
        arrive(rows_ref.at[r, q], row_sem.at[r, q])

    def wait_col(zr, q):
        arrive(cols_ref.at[zr, q], col_sem.at[zr, q])

    def relays(c):
        source = rows_ref.at[0, 2 + c]
        return [
            remote(source, cols_ref.at[2, 2], relay_send.at[c, 1], col_sem.at[2, 2], device(mirror, x, y, cores[c])),
            remote(source, cols_ref.at[1, 2], relay_send.at[c, 0], col_sem.at[1, 2], device(z, nx_, y, cores[c])),
            remote(source, cols_ref.at[0, 3 - c], relay_send.at[c, 3], col_sem.at[0, 3 - c], sibling),
        ]

    def at_home(c):
        return pltpu.make_async_copy(rows_ref.at[0, 2 + c], cols_ref.at[0, 2 + c], home_sem.at[c])

    def across(r, c):
        return remote(rows_ref.at[r, c], rows_ref.at[1 - r, 2 + c], relay_send.at[c, r], row_sem.at[1 - r, 2 + c],
                      device(z, x, ny_, k))

    @pl.when(owner)
    def _():
        for c in range(2):
            wait_row(0, 2 + c)
            for copy in relays(c):
                copy.start()
            at_home(c).start()

    @pl.when(other)
    def _():
        for r in (1, 0):
            for c in range(2):
                wait_row(r, c)
                across(r, c).start()

    places = (z * nx + x, z * nx + nx_, mirror * nx + x, mirror * nx + nx_)

    def tally(t, carry):
        a, b = ti_ref[t], tj_ref[t]
        result = []
        for zr, j in enumerate(places):
            ahead = jnp.where(a == block, 1, 0) * jnp.where(b == j, 1, 0)
            behind = jnp.where(b == block, 1, 0) * jnp.where(a == j, 1, 0)
            result += [carry[2 * zr] + ahead, carry[2 * zr + 1] + behind]
        return tuple(result)

    tallies = lax.fori_loop(0, tasks, tally, (jnp.int32(0),) * (2 * nz))
    ahead = [tallies[2 * zr].astype(jnp.float32) for zr in range(nz)]
    weight = [(tallies[2 * zr] + tallies[2 * zr + 1]).astype(jnp.float32) for zr in range(nz)]
    spread = jnp.broadcast_to(vir_ref[...].reshape(1, virtuals), vsum.shape)
    vsum[...] = spread + spread.T

    def pass_on(zr, a, slot):
        q = 2 * a
        return remote(cols_ref.at[zr, q], cols_ref.at[zr, q + 1], pass_send.at[slot], col_sem.at[zr, q + 1], sibling)

    passed = []

    def launch(copy):
        copy.start()
        passed.append(copy)

    def take(zr, a):
        q = 2 * a
        wait_col(zr, q)
        if zr == 2:
            launch(remote(cols_ref.at[2, q], cols_ref.at[3, q], pass_send.at[len(passed)], col_sem.at[3, q],
                          device(z, nx_, y, k)))
        launch(pass_on(zr, a, len(passed)))

    def amplitudes(r, zr):
        kij = jnp.dot(flips[r], cols_ref[zr].reshape(aux, virtuals), preferred_element_type=jnp.float32)
        pair = occ_ref[block * 2 + lax.rem(y + r, 2)] + occ_ref[places[zr] * 2 + y]
        amp[zr, r] = ((2.0 * kij - kij.T) / (pair - vsum[...])).astype(jnp.bfloat16)

    take(1, 0)
    take(2, 0)
    take(1, 1)
    take(2, 1)

    @pl.when(owner)
    def _():
        wait_row(0, 1)

    @pl.when(other)
    def _():
        for c in range(2):
            wait_row(0, 2 + c)

    flips[0] = rows_ref[0].reshape(aux, virtuals).T
    wait_col(0, 1)

    @pl.when(owner)
    def _():
        for c in range(2):
            at_home(c).wait()

    @pl.when(other)
    def _():
        for c in range(2):
            wait_col(0, 2 + c)

    amplitudes(0, 0)
    for q in (1, 3):
        wait_col(1, q)
    amplitudes(0, 1)
    take(3, 0)
    for q in (1, 3):
        wait_col(2, q)
    amplitudes(0, 2)
    @pl.when(owner)
    def _():
        for q in (1, 2, 3):
            wait_row(1, q)

    @pl.when(other)
    def _():
        for q in (2, 3):
            wait_row(1, q)

    flips[1] = rows_ref[1].reshape(aux, virtuals).T
    for zr in range(2):
        amplitudes(1, zr)
    take(3, 1)
    for q in (1, 3):
        wait_col(3, q)
    amplitudes(0, 3)

    def gamma_sends(r, a, c):
        over_z, over_y = k == c, k == 1 - c
        q = 2 * a + c
        src, send = stage.at[r, q], gamma_send.at[r, q]
        if a == 0:
            sends = [(both(other, over_z), remote(src, xmsg.at[r], send, x_sem.at[r], device(twin, x, y, cores[c])))]
            if c == 1:
                sends.append((owner, remote(total.at[r, q], keep.at[r], send, keep_sem.at[r], sibling)))
            return sends
        return [
            (both(other, over_z), remote(src, fold.at[r], send, fold_sem.at[r], device(twin, x, y, k))),
            (both(other, over_y), remote(src, fold.at[1 - r], send, fold_sem.at[1 - r], device(z, x, ny_, k))),
            (both(owner, over_y), remote(src, ymsg.at[1 - r], send, y_sem.at[1 - r], device(z, x, ny_, cores[c]))),
        ]

    def guarded(condition, action):
        @pl.when(condition)
        def _():
            action()

    def send_off(r, a, c):
        for condition, copy in gamma_sends(r, a, c):
            guarded(condition, copy.start)

    def gamma(r, a, hold=False):
        for c in range(2):
            q = 2 * a + c
            value = weight[0] * lax.dot_general(
                cols_ref[0, q], amp[0, r], (((1,), (1,)), ((), ())), preferred_element_type=jnp.float32)
            for zr in range(1, nz):
                value += weight[zr] * lax.dot_general(
                    cols_ref[zr, q], amp[zr, r], (((1,), (1,)), ((), ())), preferred_element_type=jnp.float32)
            total[r, q] = value
            stage[r, q] = value.astype(jnp.bfloat16)
            if q == 0:
                @pl.when(owner)
                def _():
                    keep[r] = value

            if not hold:
                send_off(r, a, c)

    def folded(own, r, c):
        if own:
            return remote(stage.at[r, 2 + c], ymsg.at[1 - r], fold_send.at[r], y_sem.at[1 - r], device(z, x, ny_, cores[c]))
        return remote(stage.at[r, c], xmsg.at[r], fold_send.at[r], x_sem.at[r], device(twin, x, y, cores[c]))

    def holders(own):
        return [(c, both(owner, k == c) if own else both(other, k == 1 - c)) for c in range(2)]

    def fold_in(own, r):
        for c, condition in holders(own):
            @pl.when(condition)
            def _():
                arrive(fold.at[r], fold_sem.at[r])
                q = (2 if own else 0) + c
                stage[r, q] = (total[r, q] + fold[r].astype(jnp.float32)).astype(jnp.bfloat16)
                folded(own, r, c).start()

    gamma(0, 1)

    for zr in range(2, nz):
        amplitudes(1, zr)

    gamma(1, 1)

    def square(zr):
        return sum(lax.dot_general(amp[zr, r], amp[zr, r], (((1,), (1,)), ((), ())),
                                   preferred_element_type=jnp.float32) for r in range(2))

    dens = ahead[0] * square(0)
    for zr in range(1, nz):
        dens += ahead[zr] * square(zr)
    part[...] = dens.reshape(part.shape)
    me = x * 2 + k
    quad = []
    for dx in range(2):
        for dk in range(2):
            if dx or dk:
                tx, tk = lax.rem(x + dx, 2), lax.rem(k + dk, 2)
                quad.append((dx * 2 + dk, tx * 2 + tk, device(z, tx, y, tk)))
    line = [(slot, dz, device(dz, x, y, k)) for slot, dz in ((1, twin), (2, mirror), (3, nz - 1 - twin))]
    pair = remote(plane.at[5], plane.at[4], plane_send.at[3], plane_sem.at[4], device(z, x, ny_, k))

    def scatter(slot, there, where):
        return remote(part.at[there], gath.at[slot], part_send.at[slot - 1], part_sem.at[slot], where)

    def swap(slot, dz, where):
        return remote(strip.at[dz], plane.at[slot], plane_send.at[slot - 1], plane_sem.at[slot], where)

    def collect(slot, dz, where):
        return remote(dens_ref.at[me, z], dens_ref.at[me, z], col_send.at[slot - 1], line_sem.at[z], where)

    def spread_out(slot, there, where):
        return remote(dens_ref.at[me], dens_ref.at[me], dens_send.at[slot - 1], dens_sem.at[me], where)

    for item in quad:
        scatter(*item).start()
    gath[0] = part[me]
    gamma(0, 0, True)
    for slot, there, where in quad:
        arrive(gath.at[slot], part_sem.at[slot])
    strip[...] = (gath[0] + gath[1]) + (gath[2] + gath[3])
    for item in line:
        swap(*item).start()
    plane[0] = strip[z]
    for c in range(2):
        send_off(0, 0, c)
    fold_in(True, 0)
    gamma(1, 0)
    for slot, dz, where in line:
        arrive(plane.at[slot], plane_sem.at[slot])
    plane[5] = (plane[0] + plane[1]) + (plane[2] + plane[3])
    pair.start()
    arrive(plane.at[4], plane_sem.at[4])
    dens_ref[me, z] = (plane[4] + plane[5]) * (1.0 / tasks)
    for item in line:
        collect(*item).start()
    fold_in(False, 1)
    fold_in(True, 1)
    fold_in(False, 0)
    for slot, dz, where in line:
        arrive(dens_ref.at[me, dz], line_sem.at[dz])
    for item in quad:
        spread_out(*item).start()

    for r in (1, 0):
        guarded(other, lambda: arrive(keep.at[r], keep_sem.at[r]))
        arrive(xmsg.at[r], x_sem.at[r])
        arrive(ymsg.at[r], y_sem.at[r])
        for at in range(2):
            @pl.when(y == at)
            def _():
                out_ref[:, (at + r) % 2, :] = (keep[r] + xmsg[r].astype(jnp.float32)) + ymsg[r].astype(jnp.float32)

    for slot, there, where in quad:
        arrive(dens_ref.at[there], dens_sem.at[there])
    for copy in opening + passed:
        copy.wait_send()

    @pl.when(other)
    def _():
        for copy in home:
            copy.wait_send()
        for r in range(2):
            for c in range(2):
                across(r, c).wait_send()

    @pl.when(owner)
    def _():
        for c in range(2):
            for copy in relays(c):
                copy.wait_send()

    for r in range(2):
        for a in range(2):
            for c in range(2):
                for condition, copy in gamma_sends(r, a, c):
                    guarded(condition, copy.wait_send)
    for own in (True, False):
        for c, condition in holders(own):
            for r in range(2):
                guarded(condition, folded(own, r, c).wait_send)
    for item in quad:
        scatter(*item).wait_send()
        spread_out(*item).wait_send()
    for item in line:
        swap(*item).wait_send()
        collect(*item).wait_send()
    pair.wait_send()


def fused(integrals, occ_count, occ_energy, vir_energy, task_iblock, task_jblock, nz, nx):
    aux_local, orbitals, virtuals = integrals.shape
    aux = aux_local * lax.axis_size("ocol")
    tasks = task_jblock.shape[0]
    share = virtuals // (4 * nz)
    half, full = jnp.bfloat16, jnp.float32
    dma = pltpu.SemaphoreType.DMA
    vmem, smem = pl.BlockSpec(memory_space=pltpu.VMEM), pl.BlockSpec(memory_space=pltpu.SMEM)
    out, dens = pl.pallas_call(
        functools.partial(fused_kernel, nz, nx, tasks),
        out_shape=[
            jax.ShapeDtypeStruct((aux_local, orbitals, virtuals), full),
            jax.ShapeDtypeStruct((4, nz, share, virtuals), full),
        ],
        in_specs=[vmem, smem, smem, smem, smem, vmem],
        out_specs=[vmem, vmem],
        scratch_shapes=[
            pltpu.VMEM((2, aux_local, virtuals), half),
            pltpu.VMEM((2, 4, aux_local, virtuals), half),
            pltpu.VMEM((nz, 4, aux_local, virtuals), half),
            pltpu.VMEM((2, virtuals, aux), half),
            pltpu.VMEM((virtuals, virtuals), full),
            pltpu.VMEM((nz, 2, virtuals, virtuals), half),
            pltpu.VMEM((2, 4, aux_local, virtuals), full),
            pltpu.VMEM((2, 4, aux_local, virtuals), half),
            pltpu.VMEM((2, aux_local, virtuals), half),
            pltpu.VMEM((2, aux_local, virtuals), half),
            pltpu.VMEM((2, aux_local, virtuals), full),
            pltpu.VMEM((2, aux_local, virtuals), half),
            pltpu.VMEM((4, nz, share, virtuals), full),
            pltpu.VMEM((4, nz, share, virtuals), full),
            pltpu.VMEM((nz, share, virtuals), full),
            pltpu.VMEM((nz + 2, share, virtuals), full),
            dma((2, 4)), dma((nz, 4)), dma((2,)), dma((2,)), dma((2,)), dma((2,)), dma((4,)), dma((2 * nz,)), dma((nz,)), dma((4,)),
            dma((9,)), dma((2, 4)), dma((8,)), dma((2, 4)), dma((2,)), dma((3,)), dma((2 * nz - 1,)), dma((nz - 1,)), dma((3,)), dma((2,)),
        ],
        compiler_params=pltpu.CompilerParams(
            collective_id=3, has_side_effects=True, vmem_limit_bytes=56 * 1024 * 1024),
    )(jnp.transpose(integrals, (1, 0, 2)), occ_count, occ_energy, task_iblock[:, 0], task_jblock, vir_energy)
    return out, dens.reshape(virtuals, virtuals)


def local(integrals, occ_count, occ_energy, vir_energy, task_iblock, task_jblock):
    aux_local, orbitals, virtuals = integrals.shape
    span = orbitals * virtuals
    blocks = lax.axis_size("orow")
    cols = lax.axis_size("ocol")
    if blocks == 8 and cols == 4 and orbitals == 2:
        return fused(integrals, occ_count, occ_energy, vir_energy, task_iblock, task_jblock, blocks // 2, 2)
    row = lax.axis_index("orow")
    col = lax.axis_index("ocol")
    aux = aux_local * cols
    active = jnp.arange(orbitals) < occ_count[row]
    masked = integrals * active.astype(jnp.bfloat16)[None, :, None]
    shard = masked.reshape(aux_local, span)
    gathered = gather_all(shard).reshape(blocks, aux, span)
    i_list, j_list = task_iblock[:, 0], task_jblock
    ids = jnp.arange(blocks)
    i_hot = i_list[None, :] == ids[:, None]
    j_hot = j_list[None, :] == ids[:, None]
    first = jnp.sum((i_list == row)[None, :] & j_hot, axis=1).astype(jnp.int32)
    second = jnp.sum((j_list == row)[None, :] & i_hot, axis=1).astype(jnp.int32)
    numbers = jnp.concatenate([jnp.stack([row, col]).astype(jnp.int32), first + second, first])
    gamma, dens = pl.pallas_call(
        functools.partial(pair_kernel, orbitals, cols),
        grid_spec=pltpu.PrefetchScalarGridSpec(
            num_scalar_prefetch=2,
            grid=(blocks,),
            in_specs=[
                pl.BlockSpec((1, aux, span), lambda s, num, occ: (num[0], 0, 0)),
                pl.BlockSpec((1, aux, span), lambda s, num, occ: (s, 0, 0)),
                pl.BlockSpec((1, aux_local, span), lambda s, num, occ: (s, num[1], 0)),
                pl.BlockSpec((1, virtuals), lambda s, num, occ: (0, 0)),
                pl.BlockSpec((virtuals, 1), lambda s, num, occ: (0, 0)),
            ],
            out_specs=[
                pl.BlockSpec((aux_local, span), lambda s, num, occ: (0, 0)),
                pl.BlockSpec((virtuals // cols, virtuals), lambda s, num, occ: (0, 0)),
            ],
            scratch_shapes=[pltpu.VMEM((span, aux), jnp.bfloat16), pltpu.VMEM((orbitals, virtuals, span), jnp.bfloat16)],
        ),
        out_shape=[
            jax.ShapeDtypeStruct((aux_local, span), jnp.float32),
            jax.ShapeDtypeStruct((virtuals // cols, virtuals), jnp.float32),
        ],
        compiler_params=pltpu.CompilerParams(vmem_limit_bytes=56 * 1024 * 1024),
    )(numbers, occ_energy, gathered, gathered, gathered, vir_energy[None, :], vir_energy[:, None])
    density = sum_density(dens, i_list.shape[0])
    return gamma.reshape(aux_local, orbitals, virtuals), density


def solution(mesh):
    return jax.shard_map(
        local,
        mesh=mesh,
        in_specs=(P("ocol", "orow", None), P(), P(), P(), P(), P()),
        out_specs=(P("ocol", "orow", None), P()),
        check_vma=False,
    )
```
